32 devices in a mesh: lon: 8 (over z, core), mem: 4 (over y, x).
Axes of the slice: x: 2, y: 2, z: 4, core: 2. Of those that a mesh axis runs over, the one named last changes fastest.
Arguments:
- members: float32 [32, 4, 192, 256], P('mem', None, 'lon'), may hold values from -6 to 6
- courant_lon: float32 [4, 192, 256], P(None, 'lon'), may hold values from -0.55 to 0.55
- courant_lat: float32 [4, 192, 256], P(None, 'lon'), may hold values from -0.4 to 0.4
- vert_modes: float32 [2, 4], replicated, may hold values from -1 to 1
- horiz_modes: float32 [4, 192, 256], P(None, 'lon'), may hold values from -1 to 1
- obs_index: int32 [16384], P('lon'), may hold values from 0 to 24575
- obs_count: int32 [8], P('lon'), may hold values from 1024 to 2048, as said below
- obs_value: float32 [16384], P('lon'), may hold values from -6 to 6
- obs_var: float32 [16384], P('lon'), may hold values from 2 to 48
Outputs:
- prior_trajectories: float32 [32, 4, 192, 256], P('mem', None, 'lon')
- analysis_mean: float32 [4, 192, 256], P(None, 'lon')
The draws below stay inside these ranges and needn't reach their ends.
Inputs may be any that keep to these rules, and one draw needn't show every extreme that they name: `obs_index`: index of a cell within the band's own block: level, then longitude within the band, then latitude. Each band uses its first obs_count slots; some band uses all 2048.
All inputs are finite; a program needn't handle non-finite values.
Results may differ from the reference program's by a relative error of at most 0.0001.
Values sent between devices are 32-bit elements; how exact they have to be, the bound alone decides.
A program may use at most 128 MiB of HBM per device.

```python
import math
import jax
import jax.numpy as jnp
from jax import lax

LON_DEV = 24
NLAT = 256
L = 4
KV = 2
KH = 4
ADV_STEPS = 2
OBS_DEV = 2048
NLON = 192
BANDS = 8
MEMBERS = 32
NOBS = 16384


def draw_obs_count(key, part):
    key_count, key_full = jax.random.split(key)
    counts = jax.random.randint(key_count, (BANDS,), OBS_DEV // 2, OBS_DEV + 1)
    full_band = jax.random.randint(key_full, (), 0, BANDS)
    return jnp.where(jnp.arange(BANDS) == full_band, OBS_DEV, counts).astype(jnp.int32)


def draw_obs_var(key, part):
    band_pos = (jnp.arange(NOBS) // OBS_DEV).astype(jnp.float32)
    rise_factor = 1.0 + 2.0 * band_pos / max(BANDS - 1, 1)
    spread = jnp.exp(jax.random.uniform(key, (NOBS,), jnp.float32, math.log(2.0), math.log(16.0)))
    return (rise_factor * spread).astype(jnp.float32)


def set_ends(values, rng, least, largest):
    place = [jax.random.randint(jax.random.fold_in(rng, axis), (), 0, length) for axis, length in enumerate(values.shape)]
    main_axis = values.shape.index(max(values.shape))
    next_to = place[:main_axis] + [(place[main_axis] + 1) % values.shape[main_axis]] + place[main_axis + 1:]
    return values.at[tuple(place)].set(least).at[tuple(next_to)].set(largest)


def block_scale(own_key, dims, pieces, low, high):
    def one(position, shards_of):
        draws = jax.random.uniform(jax.random.fold_in(jax.random.fold_in(own_key, 6), position), (shards_of,), jnp.float32, low / len(pieces), high / len(pieces))
        return jnp.repeat(jnp.exp(draws), dims[position] // shards_of).reshape((-1,) + (1,) * (len(dims) - position - 1))

    level = one(*pieces[0])
    for cut in pieces[1:]:
        level = level * one(*cut)
    return level


def normal_values(stream_key, extent, width, bound, pieces=(), kind=jnp.bfloat16):
    values = jax.random.normal(stream_key, extent, jnp.float32) * width
    if len(pieces) > 0:
        values = block_scale(stream_key, extent, pieces, -0.22, 0.18) * values
    return jnp.clip(values, min=-bound, max=bound).astype(kind)


def setup_inputs(seed: int = 0) -> dict:
    arg_keys = jax.random.split(jax.random.key(seed), 10)
    return {
        "members": normal_values(arg_keys[0], (MEMBERS, L, NLON, NLAT), 1.0, 6.0, ((0, 4), (2, 8)), jnp.float32),
        "courant_lon": jnp.clip(jax.random.uniform(arg_keys[1], (L, NLON, NLAT), jnp.float32, -0.55, 0.55) * block_scale(arg_keys[1], (L, NLON, NLAT), ((1, 8),), -0.4, 0.0), -0.55, 0.55),
        "courant_lat": jnp.clip(jax.random.uniform(arg_keys[2], (L, NLON, NLAT), jnp.float32, -0.4, 0.4) * block_scale(arg_keys[2], (L, NLON, NLAT), ((1, 8),), -0.4, 0.0), -0.4, 0.4),
        "vert_modes": jnp.clip(jax.random.uniform(arg_keys[3], (KV, L), jnp.float32, -1.0, 1.0), -1.0, 1.0),
        "horiz_modes": jnp.clip(jax.random.uniform(arg_keys[4], (KH, NLON, NLAT), jnp.float32, -1.0, 1.0) * block_scale(arg_keys[4], (KH, NLON, NLAT), ((1, 8),), -0.4, 0.0), -1.0, 1.0),
        "obs_index": set_ends(jax.random.randint(arg_keys[5], (NOBS,), 0, L * LON_DEV * NLAT), jax.random.fold_in(arg_keys[5], 1), 0, (L * LON_DEV * NLAT) - 1).astype(jnp.int32),
        "obs_count": draw_obs_count(jax.random.fold_in(arg_keys[9], 71), 0),
        "obs_value": normal_values(arg_keys[7], (NOBS,), 1.0, 6.0, ((0, 8),), jnp.float32),
        "obs_var": draw_obs_var(jax.random.fold_in(arg_keys[9], 71), 0),
    }


def update(centre, western, eastern, flow_lon, flow_lat):
    zero_col = jnp.zeros_like(centre[..., :1])
    south_boundary = jnp.concatenate([zero_col, centre[..., :-1]], axis=-1)
    northern = jnp.concatenate([centre[..., 1:], zero_col], axis=-1)
    result = centre - jnp.maximum(flow_lon, 0.0) * (centre - western)
    result = result - jnp.minimum(flow_lon, 0.0) * (eastern - centre)
    result = result - jnp.maximum(flow_lat, 0.0) * (centre - south_boundary)
    result = result - jnp.minimum(flow_lat, 0.0) * (northern - centre)
    return result

def reference(members, courant_lon, courant_lat, vert_modes, horiz_modes, obs_index, obs_count, obs_value, obs_var):
    prognostic_vector = members
    for section in range(ADV_STEPS):
        prognostic_vector = update(prognostic_vector, jnp.roll(prognostic_vector, 1, axis=2), jnp.roll(prognostic_vector, -1, axis=2), courant_lon, courant_lat)
    prior_trajectories = prognostic_vector
    sample_tally_overall = members.shape[0]
    lat_rows = members.shape[3]
    sample_centroid = jnp.sum(prior_trajectories, axis=0) / sample_tally_overall
    sample_departure = prior_trajectories - sample_centroid[None]
    norm_scale = (sample_tally_overall - 1) ** (-0.5)
    obs_slots = obs_index.shape[0]
    slot_idx = jnp.arange(obs_slots, dtype=jnp.int32)
    band_idx = slot_idx // OBS_DEV
    band_cells = LON_DEV * lat_rows
    level_idx = obs_index // band_cells
    within = obs_index % band_cells
    lon_global = band_idx * LON_DEV + within // lat_rows
    lat_idx = within % lat_rows
    anomaly_obs = sample_departure[:, level_idx, lon_global, lat_idx]
    mean_obs = sample_centroid[level_idx, lon_global, lat_idx]
    vert_obs = vert_modes[:, level_idx]
    horiz_obs = horiz_modes[:, lon_global, lat_idx]
    modes_obs = (vert_obs[:, None, :] * horiz_obs[None, :, :]).reshape(KV * KH, obs_slots)
    live_mask = (slot_idx % OBS_DEV < obs_count[band_idx]).astype(jnp.float32)
    obs_perts = anomaly_obs[:, None, :] * modes_obs[None, :, :] * (live_mask * norm_scale)[None, None, :]
    obs_perts = obs_perts.reshape(sample_tally_overall * KV * KH, obs_slots)
    inv_var = live_mask / obs_var
    innovation = obs_value - mean_obs
    gram_matrix = jnp.dot(obs_perts * inv_var[None, :], obs_perts.T, precision=lax.Precision.HIGHEST)
    right_side = jnp.dot(obs_perts, inv_var * innovation, precision=lax.Precision.HIGHEST)
    system = jnp.eye(gram_matrix.shape[0], dtype=jnp.float32) + gram_matrix
    factor = jnp.linalg.cholesky(system)
    weights = jax.scipy.linalg.cho_solve((factor, True), right_side)
    w_mat = weights.reshape(sample_tally_overall, KV * KH)
    mode_coef = jnp.einsum('mk,mlij->klij', w_mat, sample_departure, precision=lax.Precision.HIGHEST)
    mode_coef = mode_coef.reshape(KV, KH, mode_coef.shape[1], mode_coef.shape[2], mode_coef.shape[3])
    posterior_adjustment = jnp.einsum('al,bij,ablij->lij', vert_modes, horiz_modes, mode_coef, precision=lax.Precision.HIGHEST) * norm_scale
    return (prior_trajectories, sample_centroid + posterior_adjustment)
```

```python
import functools

import jax
import jax.numpy as jnp
from jax import lax
from jax.experimental import pallas as pl
from jax.experimental.pallas import tpu as pltpu
from jax.sharding import PartitionSpec as P

KV = 2
KH = 4
ADV_STEPS = 2
MODES = KV * KH
PAIRS = ((0, 0), (0, 1), (1, 1))
MESH = pl.DeviceIdType.MESH
VMEM_LIMIT = 24 * 1024 * 1024
HIGHEST = lax.Precision.HIGHEST
PIECE = 256
GROUPS = 4


def vmem():
    return pl.BlockSpec(memory_space=pltpu.VMEM)


def smem():
    return pl.BlockSpec(memory_space=pltpu.SMEM)


def hbm():
    return pl.BlockSpec(memory_space=pltpu.HBM)


def stay(x):
    return pltpu.with_memory_space_constraint(x, pltpu.HBM)


def greet(peers):
    barrier = pltpu.get_barrier_semaphore()
    for peer in peers:
        pl.semaphore_signal(barrier, inc=1, device_id=peer, device_id_type=MESH)
    return barrier


def axis_peers(axis, count):
    me = lax.axis_index(axis)
    return [{axis: lax.rem(me + d, count)} for d in range(1, count)]


def send(src, dst, send_sem, recv_sem, peer):
    copy = pltpu.make_async_remote_copy(
        src_ref=src, dst_ref=dst, send_sem=send_sem, recv_sem=recv_sem,
        device_id=peer, device_id_type=MESH,
    )
    copy.start()
    return copy


def bring(src, dst, sem):
    copy = pltpu.make_async_copy(src, dst, sem)
    copy.start()
    return copy


def two_terms(x):
    high = x.astype(jnp.bfloat16)
    return high, (x - high.astype(jnp.float32)).astype(jnp.bfloat16)


def front_kernel(
    n_lon, n_mem,
    members, cx, cy, horiz, index,
    prior, obs_prior, obs_horiz,
    ext, cx_ext, cy_ext, modes, cells, edge_out, edge_in, spots, terms, gathered,
    in_sem, edge_send, edge_recv, obs_send, obs_recv,
):
    mem_dev, layers, width, lats = members.shape
    stack = mem_dev * layers
    slots = index.shape[1]
    tiles = width // 8
    shift = lats.bit_length() - 1
    me = lax.axis_index("lon")
    me_mem = lax.axis_index("mem")
    left = {"lon": lax.rem(me + n_lon - 1, n_lon)}
    right = {"lon": lax.rem(me + 1, n_lon)}
    others = axis_peers("mem", n_mem)

    fields = [
        bring(members.at[m], ext.at[pl.ds(m * layers, layers), pl.ds(0, width), :], in_sem.at[m])
        for m in range(mem_dev)
    ]
    flows = [
        bring(cx, cx_ext.at[:, pl.ds(0, width), :], in_sem.at[mem_dev]),
        bring(cy, cy_ext.at[:, pl.ds(0, width), :], in_sem.at[mem_dev + 1]),
    ]
    places = bring(index, cells, in_sem.at[mem_dev + 2])
    shapes = bring(horiz, modes, in_sem.at[mem_dev + 3])
    barrier = greet([left, right] + others)
    for copy in fields + flows:
        copy.wait()
    for side, (first, second, rim) in enumerate(((0, 1, 0), (width - 2, width - 1, width - 1))):
        edge_out[side, 0:stack, :] = ext[:, first, :]
        edge_out[side, stack : 2 * stack, :] = ext[:, second, :]
        edge_out[side, 2 * stack : 2 * stack + layers, :] = cx_ext[:, rim, :]
        edge_out[side, 2 * stack + layers : 2 * stack + 2 * layers, :] = cy_ext[:, rim, :]
    pl.semaphore_wait(barrier, 2 + len(others))
    to_left = send(edge_out.at[0], edge_in.at[1], edge_send.at[0], edge_recv.at[1], left)
    to_right = send(edge_out.at[1], edge_in.at[0], edge_send.at[1], edge_recv.at[0], right)

    places.wait()
    shapes.wait()
    sub = lax.broadcasted_iota(jnp.int32, (8, 128), 0)
    lat_row = lax.broadcasted_iota(jnp.int32, (lats, PIECE), 0)

    def rows_of(start):
        return jnp.broadcast_to(lax.shift_right_logical(cells[:, pl.ds(start, 128)], shift), (8, 128))

    def picked(found, tile, wanted, blocks, origin):
        total = [jnp.zeros((8, 128), jnp.float32)] * blocks
        for t, rows in wanted:
            here = tile == t
            total = [
                jnp.where(here, found[rows + origin(k) : rows + origin(k) + 8], x)
                for k, x in enumerate(total)
            ]
        return total

    def settle(values, sublane):
        here = sub == sublane
        sums = [jnp.sum(jnp.where(here, x, 0.0), axis=0, keepdims=True) for x in values]
        while len(sums) < 8:
            sums.append(jnp.zeros((1, 128), jnp.float32))
        return jnp.concatenate(sums, axis=0)

    mode_terms = jnp.concatenate(two_terms(modes[...].reshape(KH * width, lats)), axis=1)

    def spot(c, carry):
        start = pl.multiple_of(c * PIECE, PIECE)
        lat = jnp.bitwise_and(cells[:, pl.ds(start, PIECE)], lats - 1)
        mask = jnp.where(lat_row == lat, 1.0, 0.0).astype(jnp.bfloat16)
        spots[0:lats, pl.ds(start, PIECE)] = mask
        spots[lats : 2 * lats, pl.ds(start, PIECE)] = mask
        found = jnp.dot(
            mode_terms, jnp.concatenate([mask, mask], axis=0), preferred_element_type=jnp.float32
        )
        for h in range(PIECE // 128):
            low = pl.multiple_of(start + h * 128, 128)
            row = rows_of(low)
            for l in range(1, layers):
                row = jnp.where(rows_of(low) >= l * width, rows_of(low) - l * width, row)
            tile = lax.shift_right_logical(row, 3)
            part = found[:, h * 128 : (h + 1) * 128]
            values = picked(part, tile, [(t, t * 8) for t in range(tiles)], KH, lambda k: k * width)
            obs_horiz[:, pl.ds(low, 128)] = settle(values, jnp.bitwise_and(row, 7))
        return carry

    lax.fori_loop(0, slots // PIECE, spot, 0)

    to_left.wait_recv()
    to_right.wait_recv()
    ext_rows = width + 8
    last = ext_rows - 1
    ext[:, last - 1, :] = edge_in[0, 0:stack, :]
    ext[:, last, :] = edge_in[0, stack : 2 * stack, :]
    ext[:, width, :] = edge_in[1, 0:stack, :]
    ext[:, width + 1, :] = edge_in[1, stack : 2 * stack, :]
    for side, row in ((0, last), (1, width)):
        cx_ext[:, row, :] = edge_in[side, 2 * stack : 2 * stack + layers, :]
        cy_ext[:, row, :] = edge_in[side, 2 * stack + layers : 2 * stack + 2 * layers, :]

    lane = lax.broadcasted_iota(jnp.int32, (ext_rows, lats), 1)
    for l in range(layers):
        cx_l = cx_ext[l]
        cy_l = cy_ext[l]
        east_flow = jnp.maximum(cx_l, 0.0)
        west_flow = jnp.minimum(cx_l, 0.0)
        north_flow = jnp.maximum(cy_l, 0.0)
        south_flow = jnp.minimum(cy_l, 0.0)

        def step(pair, carry, l=l, flows=(east_flow, west_flow, north_flow, south_flow)):
            inner = []
            for k in range(2):
                m = pair * 2 + k
                q = ext[m * layers + l]
                for _ in range(ADV_STEPS):
                    qw = pltpu.roll(q, 1, 0)
                    qe = pltpu.roll(q, ext_rows - 1, 0)
                    qs = jnp.where(lane == 0, 0.0, pltpu.roll(q, 1, 1))
                    qn = jnp.where(lane == lats - 1, 0.0, pltpu.roll(q, lats - 1, 1))
                    r = q - flows[0] * (q - qw)
                    r = r - flows[1] * (qe - q)
                    r = r - flows[2] * (q - qs)
                    q = r - flows[3] * (qn - q)
                inner.append(q[0:width, :])
                prior[l, m] = q[0:width, :]
            start = pl.multiple_of((l * mem_dev + pair * 2) * width, 16)
            high, low = two_terms(jnp.concatenate(inner, axis=0))
            terms[pl.ds(start, 2 * width), 0:lats] = high
            terms[pl.ds(start, 2 * width), lats : 2 * lats] = low
            return carry

        lax.fori_loop(0, mem_dev // 2, step, 0, unroll=2)

    wanted = [(l * tiles + t, l * mem_dev * width + t * 8) for l in range(layers) for t in range(tiles)]

    def gather(c, carry):
        start = pl.multiple_of(c * PIECE, PIECE)
        found = jnp.dot(
            terms[...], spots[:, pl.ds(start, PIECE)], preferred_element_type=jnp.float32
        )
        for h in range(PIECE // 128):
            low = pl.multiple_of(start + h * 128, 128)
            row = rows_of(low)
            part = found[:, h * 128 : (h + 1) * 128]
            tile = lax.shift_right_logical(row, 3)
            values = picked(part, tile, wanted, mem_dev, lambda k: k * width)
            gathered[me_mem, :, pl.ds(low, 128)] = settle(values, jnp.bitwise_and(row, 7))
        return carry

    span = slots // GROUPS
    steps = span // PIECE
    copies = []
    for c in range(GROUPS):
        lax.fori_loop(c * steps, (c + 1) * steps, gather, 0)
        piece = gathered.at[me_mem, :, pl.ds(c * span, span)]
        for d, peer in enumerate(others):
            copies.append(send(piece, piece, obs_send.at[c, d], obs_recv.at[c, d], peer))
    for copy in copies:
        copy.wait_recv()
    obs_prior[...] = gathered[...]
    to_left.wait_send()
    to_right.wait_send()
    for copy in copies:
        copy.wait_send()


def gram_kernel(
    n_lon, n_mem, norm,
    obs_prior, obs_horiz, prior, index, value_in, var_in, vert_in, count,
    system, level,
    cells, value, var, vert, total, staged, heard,
    in_sem, part_send, part_recv, all_send, all_recv, level_send, level_recv,
):
    layers, mem_dev, width, lats = prior.shape
    slots = index.shape[1]
    members = n_mem * mem_dev
    me = lax.axis_index("lon")
    me_mem = lax.axis_index("mem")
    lon_peers = axis_peers("lon", n_lon)
    mem_peers = axis_peers("mem", n_mem)

    arrive = [
        bring(src, dst, in_sem.at[i])
        for i, (src, dst) in enumerate(
            ((index, cells), (value_in, value), (var_in, var), (vert_in, vert))
        )
    ]
    barrier = greet(lon_peers + mem_peers)
    for copy in arrive:
        copy.wait()
    total[...] = jnp.zeros_like(total)
    span = slots // GROUPS
    slot = lax.broadcasted_iota(jnp.int32, (1, span), 1)
    sub = lax.broadcasted_iota(jnp.int32, (8, span), 0)
    factors = [[jnp.broadcast_to(vert[a : a + 1, l : l + 1], (1, span)) for l in range(layers)] for a in range(KV)]
    contract = (((1,), (1,)), ((), ()))

    def part(c, carry):
        start = pl.multiple_of(c * span, span)
        at = pl.ds(start, span)
        states = obs_prior[:, :, at].reshape(members, span)
        centre = jnp.sum(states, axis=0, keepdims=True) / members
        anomaly = states - centre
        mine = obs_prior[me_mem, :, at] - centre
        cell = cells[:, at]
        v = []
        for a in range(KV):
            x = factors[a][0]
            for l in range(1, layers):
                x = jnp.where(cell >= l * width * lats, factors[a][l], x)
            v.append(x)
        inv_var = jnp.where(slot + start < count[0], 1.0, 0.0) / var[:, at]
        drive = inv_var * (value[:, at] - centre) * norm
        weight = inv_var * (norm * norm)
        shapes = obs_horiz[0:KH, at]
        right = jnp.concatenate([anomaly * shapes[b : b + 1] for b in range(KH)], axis=0)
        own = jnp.concatenate([mine * shapes[b : b + 1] for b in range(KH)], axis=0)
        drives = jnp.where(sub == 0, v[0] * drive, jnp.where(sub == 1, v[1] * drive, 0.0))
        left = jnp.concatenate(
            [own * (v[a] * v[e] * weight) for a, e in PAIRS] + [drives, jnp.zeros_like(drives)], axis=0
        )
        right_high, right_low = two_terms(right)
        left_high, left_low = two_terms(left)
        first = lax.dot_general(
            jnp.concatenate([left_high, left_low], axis=0), right_high, contract,
            preferred_element_type=jnp.float32,
        )
        second = lax.dot_general(
            left_high, right_low, contract, preferred_element_type=jnp.float32
        )
        rows = left.shape[0]
        total[...] += first[0:rows] + first[rows : 2 * rows] + second
        return carry

    lax.fori_loop(0, GROUPS, part, 0)
    local = KH * mem_dev
    lane = lax.broadcasted_iota(jnp.int32, (8, 128), 1)
    row = lax.broadcasted_iota(jnp.int32, (8, 128), 0)

    def block(pair, b):
        return total[pair * local + b * 8 : pair * local + b * 8 + 8, :]

    for pair in range(3):
        staged[pair] = block(pair, 0)
        staged[3 + pair] = jnp.where(lane < 32, pltpu.roll(block(pair, 3), 32, 1), block(pair, 1))
    staged[6] = jnp.where(lane < 64, pltpu.roll(block(1, 2), 64, 1), block(0, 2))
    side = total[3 * local : 3 * local + 8, :]
    other = pltpu.roll(pltpu.roll(side, 64, 1), KV, 0)
    staged[7] = jnp.where(lane < 64, jnp.where(row < KV, side, other), block(2, 2))

    pl.semaphore_wait(barrier, len(lon_peers) + len(mem_peers))
    parts = [
        send(staged.at[peer["lon"]], heard.at[me], part_send.at[d], part_recv.at[d], peer)
        for d, peer in enumerate(lon_peers)
    ]
    shares = [
        send(prior.at[peer["mem"]], level.at[me_mem], level_send.at[d], level_recv.at[d], peer)
        for d, peer in enumerate(mem_peers)
    ]
    heard[me] = staged[me]
    level[me_mem] = prior[me_mem]
    for copy in parts:
        copy.wait_recv()
    summed = heard[0]
    for d in range(1, n_lon):
        summed = summed + heard[d]
    system[me_mem, me] = summed
    spread = []
    for step in range(1, n_lon * n_mem):
        peer = {
            "lon": lax.rem(me + step // n_mem, n_lon),
            "mem": lax.rem(me_mem + step % n_mem, n_mem),
        }
        piece = system.at[me_mem, me]
        spread.append(send(piece, piece, all_send.at[step], all_recv.at[step], peer))
    for copy in spread + shares:
        copy.wait_recv()
    for copy in parts + spread + shares:
        copy.wait_send()


def unpack(system, work, size):
    lane = lax.broadcasted_iota(jnp.int32, (32, 128), 1)
    unit = jnp.where(
        lax.broadcasted_iota(jnp.int32, (128, 128), 0) == lax.broadcasted_iota(jnp.int32, (128, 128), 1),
        1.0, 0.0,
    )
    groups = system.shape[0]

    def take(t):
        return jnp.concatenate([system[g, t] for g in range(groups)], axis=0)

    last = [pltpu.roll(take(6), 64, 1), take(7)]
    thirds = [take(6), last[0], last[1]]
    for pair, (a, e) in enumerate(PAIRS):
        first, second, third = take(pair), take(3 + pair), thirds[pair]
        first_32, first_64, first_96 = (pltpu.roll(first, s, 1) for s in (96, 64, 32))
        second_32, second_64 = (pltpu.roll(second, s, 1) for s in (96, 64))
        third_32 = pltpu.roll(third, 96, 1)
        whole = jnp.concatenate(
            [
                first,
                jnp.where(lane < 32, first_32, second),
                jnp.where(lane < 32, first_64, jnp.where(lane < 64, second_32, third)),
                jnp.where(
                    lane < 32, first_96,
                    jnp.where(lane < 64, second_64, jnp.where(lane < 96, third_32, second_32)),
                ),
            ],
            axis=0,
        )
        if a == e:
            work[a * 128 : (a + 1) * 128, a * 128 : (a + 1) * 128] = whole + unit
        else:
            work[a * 128 : (a + 1) * 128, e * 128 : (e + 1) * 128] = whole
            work[e * 128 : (e + 1) * 128, a * 128 : (a + 1) * 128] = whole
    side = system[0, 7]
    turned = pltpu.roll(side, 64, 1)
    narrow = lax.broadcasted_iota(jnp.int32, (1, 128), 1)
    for a in range(KV):
        line = jnp.where(narrow < 64, side[a : a + 1], turned[KV + a : KV + a + 1])
        work[a * 128 : (a + 1) * 128, size : size + 128] = jnp.broadcast_to(line, (128, 128)).T


def solve_kernel(
    system, prior, level, horiz_in, vert_in,
    mixed, mean, horiz, prior_out,
    work, vert, sems,
):
    size = work.shape[0]
    columns = size + 128
    layers = prior.shape[0]
    keeps = [bring(prior.at[l], prior_out.at[:, l], sems.at[l]) for l in range(layers)]
    shapes = bring(horiz_in, horiz, sems.at[layers])
    factors = bring(vert_in, vert, sems.at[layers + 1])
    unpack(system, work, size)
    field = level[0, 0]
    for g in range(level.shape[0]):
        for m in range(level.shape[1]):
            if g + m > 0:
                field = field + level[g, m]
    mean[...] = field / (level.shape[0] * level.shape[1])
    depth = 64
    tile = (8, 128)
    sub = lax.broadcasted_iota(jnp.int32, tile, 0)
    outer = lax.broadcasted_iota(jnp.int32, (size, depth), 0)
    for top in range(0, size, depth):
        low = top // 128 * 128
        pieces = (columns - low) // 128
        panel = [
            [work[top + i * 8 : top + i * 8 + 8, low + k * 128 : low + (k + 1) * 128] for k in range(pieces)]
            for i in range(depth // 8)
        ]
        for s in range(depth // 8):
            lane = top - low + s * 8
            a = [jnp.broadcast_to(panel[s][0][:, lane + c : lane + c + 1], tile) for c in range(8)]
            rows = panel[s]
            for j in range(8):
                inv = 1.0 / jnp.broadcast_to(a[j][j : j + 1], tile)
                f = a[j]

                def reduce(x, j=j, inv=inv, f=f):
                    n = jnp.broadcast_to(x[j : j + 1], tile) * inv
                    return jnp.where(sub == j, n, x - f * n)

                for c in range(j + 1, 8):
                    a[c] = reduce(a[c])
                rows = [reduce(x) for x in rows]
            panel[s] = rows
            spread = [[jnp.broadcast_to(x[j : j + 1], tile) for x in rows] for j in range(8)]
            for d in range(1, depth // 8):
                i = (s + d) % (depth // 8)
                lead = panel[i][0]
                block = panel[i]
                for j in range(8):
                    f = jnp.broadcast_to(lead[:, lane + j : lane + j + 1], tile)
                    block = [x - f * y for x, y in zip(block, spread[j])]
                panel[i] = block
        for i in range(depth // 8):
            for k in range(pieces):
                work[top + i * 8 : top + i * 8 + 8, low + k * 128 : low + (k + 1) * 128] = panel[i][k]
        inside = (outer >= top) & (outer < top + depth)
        factor = jnp.where(inside, 0.0, work[:, top : top + depth])
        first = (top + depth) // 128 * 128
        work[:, first:columns] -= jnp.dot(
            factor, work[top : top + depth, first:columns],
            precision=HIGHEST, preferred_element_type=jnp.float32,
        )
    factors.wait()
    me_mem = lax.axis_index("mem")
    half = size // KV
    lines = []
    for a in range(KV):
        x = jnp.broadcast_to(vert[a : a + 1, 0:1], (1, 128))
        for l in range(1, layers):
            x = jnp.where(me_mem == l, jnp.broadcast_to(vert[a : a + 1, l : l + 1], (1, 128)), x)
        lines.append(x)
    mixed[...] = lines[0] * work[0:half, size:columns] + lines[1] * work[half:size, size:columns]
    shapes.wait()
    for keep in keeps:
        keep.wait()


def analysis_kernel(
    n_mem, norm,
    mixed, mean, level, horiz,
    analysis,
    fields, part_send, part_recv,
):
    mem_dev = level.shape[1]
    lats = mean.shape[1]
    members = n_mem * mem_dev
    me_mem = lax.axis_index("mem")
    peers = axis_peers("mem", n_mem)
    barrier = greet(peers)
    centre = mean[...]
    shapes = [horiz[b] for b in range(KH)]
    total = jnp.zeros_like(centre)
    for m in range(members):
        coef = None
        for b in range(KH):
            w = jnp.concatenate([mixed[b * members + m : b * members + m + 1, :]] * (lats // 128), axis=1)
            coef = w * shapes[b] if coef is None else coef + w * shapes[b]
        total = total + coef * (level[m // mem_dev, m % mem_dev] - centre)
    fields[me_mem] = centre + total * norm
    pl.semaphore_wait(barrier, len(peers))
    piece = fields.at[me_mem]
    copies = [
        send(piece, piece, part_send.at[d], part_recv.at[d], peer) for d, peer in enumerate(peers)
    ]
    for copy in copies:
        copy.wait_recv()
    analysis[...] = fields[...]
    for copy in copies:
        copy.wait_send()


def params(collective=None):
    if collective is None:
        return pltpu.CompilerParams(vmem_limit_bytes=VMEM_LIMIT)
    return pltpu.CompilerParams(
        vmem_limit_bytes=VMEM_LIMIT, collective_id=collective, has_side_effects=True
    )


def fast_device(
    members, courant_lon, courant_lat, vert_modes, horiz_modes,
    obs_index, obs_count, obs_value, obs_var,
):
    f32 = jnp.float32
    bf16 = jnp.bfloat16
    mem_dev, layers, width, lats = members.shape
    n_lon = lax.axis_size("lon")
    n_mem = lax.axis_size("mem")
    total = mem_dev * n_mem
    size = total * MODES
    norm = (total - 1) ** (-0.5)
    slots = obs_index.shape[0]
    stack = mem_dev * layers
    index = obs_index.reshape(1, slots)
    dma = pltpu.SemaphoreType.DMA
    edge_rows = 2 * stack + 2 * layers
    prior, obs_prior, obs_horiz = pl.pallas_call(
        functools.partial(front_kernel, n_lon, n_mem),
        out_shape=(
            jax.ShapeDtypeStruct((layers, mem_dev, width, lats), f32),
            jax.ShapeDtypeStruct((n_mem, mem_dev, slots), f32),
            jax.ShapeDtypeStruct((8, slots), f32),
        ),
        in_specs=[hbm()] * 5,
        out_specs=(vmem(),) * 3,
        scratch_shapes=[
            pltpu.VMEM((stack, width + 8, lats), f32),
            pltpu.VMEM((layers, width + 8, lats), f32),
            pltpu.VMEM((layers, width + 8, lats), f32),
            pltpu.VMEM((KH, width, lats), f32),
            pltpu.VMEM((1, slots), jnp.int32),
            pltpu.VMEM((2, edge_rows, lats), f32),
            pltpu.VMEM((2, edge_rows, lats), f32),
            pltpu.VMEM((2 * lats, slots), bf16),
            pltpu.VMEM((stack * width, 2 * lats), bf16),
            pltpu.VMEM((n_mem, mem_dev, slots), f32),
            dma((mem_dev + 4,)),
            dma((2,)), dma((2,)),
            dma((GROUPS, n_mem - 1)), dma((GROUPS, n_mem - 1)),
        ],
        compiler_params=params(1),
        name="front",
    )(*map(stay, (members, courant_lon, courant_lat, horiz_modes, index)))
    system, level = pl.pallas_call(
        functools.partial(gram_kernel, n_lon, n_mem, norm),
        out_shape=(
            jax.ShapeDtypeStruct((n_mem, n_lon, 8, 128), f32),
            jax.ShapeDtypeStruct((n_mem, mem_dev, width, lats), f32),
        ),
        in_specs=[vmem()] * 3 + [hbm()] * 4 + [smem()],
        out_specs=(vmem(), vmem()),
        scratch_shapes=[
            pltpu.VMEM((1, slots), jnp.int32),
            pltpu.VMEM((1, slots), f32),
            pltpu.VMEM((1, slots), f32),
            pltpu.VMEM((KV, layers), f32),
            pltpu.VMEM((3 * KH * mem_dev + 16, 128), f32),
            pltpu.VMEM((n_lon, 8, 128), f32),
            pltpu.VMEM((n_lon, 8, 128), f32),
            dma((4,)),
            dma((n_lon - 1,)), dma((n_lon - 1,)),
            dma((n_lon * n_mem,)), dma((n_lon * n_mem,)),
            dma((n_mem - 1,)), dma((n_mem - 1,)),
        ],
        compiler_params=params(2),
        name="gram",
    )(
        obs_prior, obs_horiz, prior,
        *map(
            stay,
            (index, obs_value.reshape(1, slots), obs_var.reshape(1, slots), vert_modes),
        ),
        obs_count,
    )
    mixed, mean, horiz, prior_out = pl.pallas_call(
        solve_kernel,
        out_shape=(
            jax.ShapeDtypeStruct((total * KH, 128), f32),
            jax.ShapeDtypeStruct((width, lats), f32),
            jax.ShapeDtypeStruct((KH, width, lats), f32),
            jax.ShapeDtypeStruct((mem_dev, layers, width, lats), f32),
        ),
        in_specs=[vmem()] * 3 + [hbm()] * 2,
        out_specs=(vmem(), vmem(), vmem(), hbm()),
        scratch_shapes=[
            pltpu.VMEM((size, size + 128), f32),
            pltpu.VMEM((KV, layers), f32),
            dma((layers + 2,)),
        ],
        compiler_params=params(),
        name="solve",
    )(system, prior, level, stay(horiz_modes), stay(vert_modes))
    analysis = pl.pallas_call(
        functools.partial(analysis_kernel, n_mem, norm),
        out_shape=jax.ShapeDtypeStruct((layers, width, lats), f32),
        in_specs=[vmem()] * 4,
        out_specs=vmem(),
        scratch_shapes=[
            pltpu.VMEM((n_mem, width, lats), f32),
            dma((n_mem - 1,)), dma((n_mem - 1,)),
        ],
        compiler_params=params(3),
        name="analysis",
    )(mixed, mean, level, horiz)
    return prior_out, analysis


def padded(block, sides, width):
    for axis, dim in sides:
        count = lax.axis_size(axis)
        forward = [(i, i + 1) for i in range(count - 1)]
        forward.append((count - 1, 0))
        backward = [(target, source) for source, target in forward]
        low = lax.ppermute(
            lax.slice_in_dim(block, block.shape[dim] - width, None, axis=dim), axis, forward
        )
        high = lax.ppermute(lax.slice_in_dim(block, 0, width, axis=dim), axis, backward)
        block = jnp.concatenate([low, block, high], axis=dim)
    return block


def update(centre, western, eastern, flow_lon, flow_lat):
    zero_col = jnp.zeros_like(centre[..., :1])
    south_boundary = jnp.concatenate([zero_col, centre[..., :-1]], axis=-1)
    northern = jnp.concatenate([centre[..., 1:], zero_col], axis=-1)
    result = centre - jnp.maximum(flow_lon, 0.0) * (centre - western)
    result = result - jnp.minimum(flow_lon, 0.0) * (eastern - centre)
    result = result - jnp.maximum(flow_lat, 0.0) * (centre - south_boundary)
    result = result - jnp.minimum(flow_lat, 0.0) * (northern - centre)
    return result


def per_device(
    members,
    courant_lon,
    courant_lat,
    vert_modes,
    horiz_modes,
    obs_index,
    obs_count,
    obs_value,
    obs_var,
):
    mem_dev, layer_tally, band_width, lat_rows = members.shape
    sample_tally_overall = mem_dev * lax.axis_size("mem")
    rim_depth = ADV_STEPS
    stacked = jnp.concatenate(
        [members.reshape(mem_dev * layer_tally, band_width, lat_rows), courant_lon, courant_lat],
        axis=0,
    )
    extended = padded(stacked, (("lon", 1),), rim_depth)
    split_at = mem_dev * layer_tally
    prognostic_vector = extended[:split_at].reshape(
        mem_dev, layer_tally, band_width + 2 * rim_depth, lat_rows
    )
    flow_lon_ext = extended[split_at : split_at + layer_tally]
    meridional_wind_padded = extended[split_at + layer_tally :]
    for section in range(rim_depth):
        out_cols = band_width + 2 * (rim_depth - 1 - section)
        first_col = section + 1
        prognostic_vector = update(
            prognostic_vector[:, :, 1 : out_cols + 1],
            prognostic_vector[:, :, 0:out_cols],
            prognostic_vector[:, :, 2 : out_cols + 2],
            flow_lon_ext[:, first_col : first_col + out_cols],
            meridional_wind_padded[:, first_col : first_col + out_cols],
        )
    sample_centroid = lax.psum(jnp.sum(prognostic_vector, axis=0), "mem") / sample_tally_overall
    sample_departure = prognostic_vector - sample_centroid[None]
    norm_scale = (sample_tally_overall - 1) ** (-0.5)
    obs_slots = obs_index.shape[0]
    band_cells = band_width * lat_rows
    level_idx = obs_index // band_cells
    within = obs_index % band_cells
    anomaly_obs = jnp.take(sample_departure.reshape(mem_dev, -1), obs_index, axis=1)
    mean_obs = jnp.take(sample_centroid.reshape(-1), obs_index)
    vert_obs = jnp.take(vert_modes, level_idx, axis=1)
    horiz_obs = jnp.take(horiz_modes.reshape(KH, -1), within, axis=1)
    modes_obs = (vert_obs[:, None, :] * horiz_obs[None, :, :]).reshape(KV * KH, obs_slots)
    live_mask = (jnp.arange(obs_slots, dtype=jnp.int32) < obs_count[0]).astype(jnp.float32)
    obs_perts = (
        anomaly_obs[:, None, :] * modes_obs[None, :, :] * (live_mask * norm_scale)[None, None, :]
    )
    obs_perts = obs_perts.reshape(mem_dev * KV * KH, obs_slots)
    inv_var = live_mask / obs_var
    innovation = obs_value - mean_obs
    all_perts = lax.all_gather(obs_perts, "mem", axis=0, tiled=True)
    gram_part = jnp.dot(all_perts * inv_var[None, :], all_perts.T, precision=lax.Precision.HIGHEST)
    side_part = jnp.dot(all_perts, inv_var * innovation, precision=lax.Precision.HIGHEST)
    gram_matrix, right_side = lax.psum((gram_part, side_part), "lon")
    system = jnp.eye(gram_matrix.shape[0], dtype=jnp.float32) + gram_matrix
    factor = jnp.linalg.cholesky(system)
    weights = jax.scipy.linalg.cho_solve((factor, True), right_side)
    w_mat = weights.reshape(sample_tally_overall, KV * KH)
    w_local = lax.dynamic_slice_in_dim(w_mat, lax.axis_index("mem") * mem_dev, mem_dev, 0)
    mode_coef = jnp.einsum(
        "mk,mlij->klij", w_local, sample_departure, precision=lax.Precision.HIGHEST
    )
    mode_coef = mode_coef.reshape(KV, KH, layer_tally, band_width, lat_rows)
    inc_part = (
        jnp.einsum(
            "al,bij,ablij->lij", vert_modes, horiz_modes, mode_coef, precision=lax.Precision.HIGHEST
        )
        * norm_scale
    )
    posterior_adjustment = lax.psum(inc_part, "mem")
    return (prognostic_vector, sample_centroid + posterior_adjustment)


def choose(*args):
    mem_dev, layers, width, lats = args[0].shape
    n_lon = lax.axis_size("lon")
    n_mem = lax.axis_size("mem")
    fits = (
        mem_dev == 8
        and layers == 4
        and n_mem == layers
        and n_lon == 8
        and width % 8 == 0
        and lats == 256
        and args[5].shape[0] % (GROUPS * PIECE) == 0
    )
    return fast_device(*args) if fits else per_device(*args)


def solution(mesh):
    placed = (
        P("mem", None, "lon", None),
        P(None, "lon", None),
        P(None, "lon", None),
        P(),
        P(None, "lon", None),
        P("lon"),
        P("lon"),
        P("lon"),
        P("lon"),
    )
    return jax.shard_map(
        choose,
        mesh=mesh,
        in_specs=placed,
        out_specs=(P("mem", None, "lon", None), P(None, "lon", None)),
        check_vma=False,
    )
```

```python
import functools

import jax
import jax.numpy as jnp
from jax import lax
from jax.experimental import pallas as pl
from jax.experimental.pallas import tpu as pltpu
from jax.sharding import PartitionSpec as P

KV = 2
KH = 4
ADV_STEPS = 2
MODES = KV * KH
PAIRS = ((0, 0), (0, 1), (1, 1))
MESH = pl.DeviceIdType.MESH
VMEM_LIMIT = 24 * 1024 * 1024
HIGHEST = lax.Precision.HIGHEST
PIECE = 256
GROUPS = 4


def vmem():
    return pl.BlockSpec(memory_space=pltpu.VMEM)


def smem():
    return pl.BlockSpec(memory_space=pltpu.SMEM)


def hbm():
    return pl.BlockSpec(memory_space=pltpu.HBM)


def stay(x):
    return pltpu.with_memory_space_constraint(x, pltpu.HBM)


def greet(peers):
    barrier = pltpu.get_barrier_semaphore()
    for peer in peers:
        pl.semaphore_signal(barrier, inc=1, device_id=peer, device_id_type=MESH)
    return barrier


def axis_peers(axis, count):
    me = lax.axis_index(axis)
    return [{axis: lax.rem(me + d, count)} for d in range(1, count)]


def send(src, dst, send_sem, recv_sem, peer):
    copy = pltpu.make_async_remote_copy(
        src_ref=src, dst_ref=dst, send_sem=send_sem, recv_sem=recv_sem,
        device_id=peer, device_id_type=MESH,
    )
    copy.start()
    return copy


def bring(src, dst, sem):
    copy = pltpu.make_async_copy(src, dst, sem)
    copy.start()
    return copy


def two_terms(x):
    high = x.astype(jnp.bfloat16)
    return high, (x - high.astype(jnp.float32)).astype(jnp.bfloat16)


def front_kernel(
    n_lon, n_mem, norm,
    members, cx, cy, horiz, index, value_in, var_in, vert_in, count,
    prior, analysis,
    level, system, work, ext, cx_ext, cy_ext, modes, cells, value, var, vert, edge_out, edge_in, spots, terms, gathered,
    obs_horiz, total, staged, heard,
    in_sem, edge_send, edge_recv, obs_send, obs_recv, far_sem,
    part_send, part_recv, all_send, all_recv, level_send, level_recv, field_send, field_recv,
):
    mem_dev, layers, width, lats = members.shape
    stack = mem_dev * layers
    slots = index.shape[1]
    tiles = width // 8
    shift = lats.bit_length() - 1
    me = lax.axis_index("lon")
    me_mem = lax.axis_index("mem")
    left = {"lon": lax.rem(me + n_lon - 1, n_lon)}
    right = {"lon": lax.rem(me + 1, n_lon)}
    others = axis_peers("mem", n_mem)

    states = [
        bring(members.at[m], ext.at[pl.ds(m * layers, layers), pl.ds(0, width), :], in_sem.at[m])
        for m in range(mem_dev)
    ]
    flows = [
        bring(cx, cx_ext.at[:, pl.ds(0, width), :], in_sem.at[mem_dev]),
        bring(cy, cy_ext.at[:, pl.ds(0, width), :], in_sem.at[mem_dev + 1]),
    ]
    places = bring(index, cells, in_sem.at[mem_dev + 2])
    shapes = bring(horiz, modes, in_sem.at[mem_dev + 3])
    observed = [
        bring(src, dst, in_sem.at[mem_dev + 4 + i])
        for i, (src, dst) in enumerate(((value_in, value), (var_in, var), (vert_in, vert)))
    ]
    barrier = greet([left, right] + others)
    for copy in states + flows:
        copy.wait()
    for side, (first, second, rim) in enumerate(((0, 1, 0), (width - 2, width - 1, width - 1))):
        edge_out[side, 0:stack, :] = ext[:, first, :]
        edge_out[side, stack : 2 * stack, :] = ext[:, second, :]
        edge_out[side, 2 * stack : 2 * stack + layers, :] = cx_ext[:, rim, :]
        edge_out[side, 2 * stack + layers : 2 * stack + 2 * layers, :] = cy_ext[:, rim, :]
    pl.semaphore_wait(barrier, 2 + len(others))
    to_left = send(edge_out.at[0], edge_in.at[1], edge_send.at[0], edge_recv.at[1], left)
    to_right = send(edge_out.at[1], edge_in.at[0], edge_send.at[1], edge_recv.at[0], right)

    places.wait()
    shapes.wait()
    sub = lax.broadcasted_iota(jnp.int32, (8, 128), 0)
    lat_row = lax.broadcasted_iota(jnp.int32, (lats, PIECE), 0)

    def rows_of(start):
        return jnp.broadcast_to(lax.shift_right_logical(cells[:, pl.ds(start, 128)], shift), (8, 128))

    def picked(found, tile, wanted, blocks, origin):
        total = [jnp.zeros((8, 128), jnp.float32)] * blocks
        for t, rows in wanted:
            here = tile == t
            total = [
                jnp.where(here, found[rows + origin(k) : rows + origin(k) + 8], x)
                for k, x in enumerate(total)
            ]
        return total

    def settle(values, sublane):
        here = sub == sublane
        sums = [jnp.sum(jnp.where(here, x, 0.0), axis=0, keepdims=True) for x in values]
        while len(sums) < 8:
            sums.append(jnp.zeros((1, 128), jnp.float32))
        return jnp.concatenate(sums, axis=0)

    mode_terms = jnp.concatenate(two_terms(modes[...].reshape(KH * width, lats)), axis=1)

    def spot(c, carry):
        start = pl.multiple_of(c * PIECE, PIECE)
        lat = jnp.bitwise_and(cells[:, pl.ds(start, PIECE)], lats - 1)
        mask = jnp.where(lat_row == lat, 1.0, 0.0).astype(jnp.bfloat16)
        spots[0:lats, pl.ds(start, PIECE)] = mask
        spots[lats : 2 * lats, pl.ds(start, PIECE)] = mask
        found = jnp.dot(
            mode_terms, jnp.concatenate([mask, mask], axis=0), preferred_element_type=jnp.float32
        )
        for h in range(PIECE // 128):
            low = pl.multiple_of(start + h * 128, 128)
            row = rows_of(low)
            for l in range(1, layers):
                row = jnp.where(rows_of(low) >= l * width, rows_of(low) - l * width, row)
            tile = lax.shift_right_logical(row, 3)
            part = found[:, h * 128 : (h + 1) * 128]
            values = picked(part, tile, [(t, t * 8) for t in range(tiles)], KH, lambda k: k * width)
            obs_horiz[:, pl.ds(low, 128)] = settle(values, jnp.bitwise_and(row, 7))
        return carry

    lax.fori_loop(0, slots // PIECE, spot, 0)

    to_left.wait_recv()
    to_right.wait_recv()
    for d in (2, n_lon - 2):
        pl.semaphore_signal(
            far_sem, inc=1, device_id={"lon": lax.rem(me + d, n_lon)}, device_id_type=MESH
        )
    ext_rows = width + 8
    last = ext_rows - 1
    ext[:, last - 1, :] = edge_in[0, 0:stack, :]
    ext[:, last, :] = edge_in[0, stack : 2 * stack, :]
    ext[:, width, :] = edge_in[1, 0:stack, :]
    ext[:, width + 1, :] = edge_in[1, stack : 2 * stack, :]
    for side, row in ((0, last), (1, width)):
        cx_ext[:, row, :] = edge_in[side, 2 * stack : 2 * stack + layers, :]
        cy_ext[:, row, :] = edge_in[side, 2 * stack + layers : 2 * stack + 2 * layers, :]

    lane = lax.broadcasted_iota(jnp.int32, (ext_rows, lats), 1)
    for l in range(layers):
        cx_l = cx_ext[l]
        cy_l = cy_ext[l]
        east_flow = jnp.maximum(cx_l, 0.0)
        west_flow = jnp.minimum(cx_l, 0.0)
        north_flow = jnp.maximum(cy_l, 0.0)
        south_flow = jnp.minimum(cy_l, 0.0)

        def step(pair, carry, l=l, flows=(east_flow, west_flow, north_flow, south_flow)):
            inner = []
            for k in range(2):
                m = pair * 2 + k
                q = ext[m * layers + l]
                for _ in range(ADV_STEPS):
                    qw = pltpu.roll(q, 1, 0)
                    qe = pltpu.roll(q, ext_rows - 1, 0)
                    qs = jnp.where(lane == 0, 0.0, pltpu.roll(q, 1, 1))
                    qn = jnp.where(lane == lats - 1, 0.0, pltpu.roll(q, lats - 1, 1))
                    r = q - flows[0] * (q - qw)
                    r = r - flows[1] * (qe - q)
                    r = r - flows[2] * (q - qs)
                    q = r - flows[3] * (qn - q)
                inner.append(q[0:width, :])
                prior[l, m] = q[0:width, :]
            start = pl.multiple_of((l * mem_dev + pair * 2) * width, 16)
            high, low = two_terms(jnp.concatenate(inner, axis=0))
            terms[pl.ds(start, 2 * width), 0:lats] = high
            terms[pl.ds(start, 2 * width), lats : 2 * lats] = low
            return carry

        lax.fori_loop(0, mem_dev // 2, step, 0, unroll=2)

    wanted = [(l * tiles + t, l * mem_dev * width + t * 8) for l in range(layers) for t in range(tiles)]

    def gather(c, carry):
        start = pl.multiple_of(c * PIECE, PIECE)
        found = jnp.dot(
            terms[...], spots[:, pl.ds(start, PIECE)], preferred_element_type=jnp.float32
        )
        for h in range(PIECE // 128):
            low = pl.multiple_of(start + h * 128, 128)
            row = rows_of(low)
            part = found[:, h * 128 : (h + 1) * 128]
            tile = lax.shift_right_logical(row, 3)
            values = picked(part, tile, wanted, mem_dev, lambda k: k * width)
            gathered[me_mem, :, pl.ds(low, 128)] = settle(values, jnp.bitwise_and(row, 7))
        return carry

    span = slots // GROUPS
    steps = span // PIECE
    copies = []
    for c in range(GROUPS):
        lax.fori_loop(c * steps, (c + 1) * steps, gather, 0)
        piece = gathered.at[me_mem, :, pl.ds(c * span, span)]
        for d, peer in enumerate(others):
            copies.append(send(piece, piece, obs_send.at[c, d], obs_recv.at[c, d], peer))
    shares = [
        send(prior.at[peer["mem"]], level.at[me_mem], level_send.at[d], level_recv.at[d], peer)
        for d, peer in enumerate(others)
    ]
    level[me_mem] = prior[me_mem]

    members_all = n_mem * mem_dev
    for copy in observed:
        copy.wait()
    slot = lax.broadcasted_iota(jnp.int32, (1, span), 1)
    head = lax.broadcasted_iota(jnp.int32, (8, span), 0)
    factors = [[jnp.broadcast_to(vert[a : a + 1, l : l + 1], (1, span)) for l in range(layers)] for a in range(KV)]
    contract = (((1,), (1,)), ((), ()))

    def part(c):
        at = pl.ds(c * span, span)
        states = gathered[:, :, at].reshape(members_all, span)
        centre = jnp.sum(states, axis=0, keepdims=True) / members_all
        anomaly = states - centre
        mine = gathered[me_mem, :, at] - centre
        cell = cells[:, at]
        v = []
        for a in range(KV):
            x = factors[a][0]
            for l in range(1, layers):
                x = jnp.where(cell >= l * width * lats, factors[a][l], x)
            v.append(x)
        inv_var = jnp.where(slot + c * span < count[0], 1.0, 0.0) / var[:, at]
        drive = inv_var * (value[:, at] - centre) * norm
        weight = inv_var * (norm * norm)
        local_modes = obs_horiz[0:KH, at]
        wide = jnp.concatenate([anomaly * local_modes[b : b + 1] for b in range(KH)], axis=0)
        own = jnp.concatenate([mine * local_modes[b : b + 1] for b in range(KH)], axis=0)
        drives = jnp.where(head == 0, v[0] * drive, jnp.where(head == 1, v[1] * drive, 0.0))
        narrow = jnp.concatenate(
            [own * (v[a] * v[e] * weight) for a, e in PAIRS] + [drives, jnp.zeros_like(drives)], axis=0
        )
        wide_high, wide_low = two_terms(wide)
        narrow_high, narrow_low = two_terms(narrow)
        first = lax.dot_general(
            jnp.concatenate([narrow_high, narrow_low], axis=0), wide_high, contract,
            preferred_element_type=jnp.float32,
        )
        second = lax.dot_general(
            narrow_high, wide_low, contract, preferred_element_type=jnp.float32
        )
        rows = narrow.shape[0]
        return first[0:rows] + first[rows : 2 * rows] + second

    peers = len(others)
    for c in range(GROUPS):
        for copy in copies[c * peers : (c + 1) * peers]:
            copy.wait_recv()
        if c == 0:
            total[...] = part(c)
        else:
            total[...] += part(c)
    local = KH * mem_dev
    lane = lax.broadcasted_iota(jnp.int32, (8, 128), 1)

    def block(pair, b):
        return total[pair * local + b * 8 : pair * local + b * 8 + 8, :]

    for pair in range(3):
        staged[pair] = block(pair, 0)
        staged[3 + pair] = jnp.where(lane < 32, pltpu.roll(block(pair, 3), 32, 1), block(pair, 1))
    staged[6] = jnp.where(lane < 64, pltpu.roll(block(1, 2), 64, 1), block(0, 2))
    side = total[3 * local : 3 * local + 8, :]
    other = pltpu.roll(pltpu.roll(side, 64, 1), KV, 0)
    staged[7] = jnp.where(lane < 64, jnp.where(sub < KV, side, other), block(2, 2))

    pl.semaphore_wait(far_sem, 2)
    parts = [
        send(staged.at[peer["lon"]], heard.at[me], part_send.at[d], part_recv.at[d], peer)
        for d, peer in enumerate(axis_peers("lon", n_lon))
    ]
    heard[me] = staged[me]
    for copy in parts:
        copy.wait_recv()
    summed = heard[0]
    for d in range(1, n_lon):
        summed = summed + heard[d]
    system[me_mem, me] = summed
    spread = []
    for hop in range(1, n_lon * n_mem):
        peer = {
            "lon": lax.rem(me + hop // n_mem, n_lon),
            "mem": lax.rem(me_mem + hop % n_mem, n_mem),
        }
        piece = system.at[me_mem, me]
        spread.append(send(piece, piece, all_send.at[hop], all_recv.at[hop], peer))
    for copy in spread:
        copy.wait_recv()

    size = members_all * MODES
    columns = size + 128
    unpack(system, work, size)
    eliminate(work, size, columns)
    half = size // KV
    lines = []
    for a in range(KV):
        x = jnp.broadcast_to(vert[a : a + 1, 0:1], (1, 128))
        for l in range(1, layers):
            x = jnp.where(me_mem == l, jnp.broadcast_to(vert[a : a + 1, l : l + 1], (1, 128)), x)
        lines.append(x)
    mixed = lines[0] * work[0:half, size:columns] + lines[1] * work[half:size, size:columns]
    for copy in shares:
        copy.wait_recv()
    centre = level[0, 0]
    for m in range(1, members_all):
        centre = centre + level[m // mem_dev, m % mem_dev]
    centre = centre / members_all
    increment = jnp.zeros_like(centre)
    for m in range(members_all):
        coef = None
        for b in range(KH):
            w = mixed[b * members_all + m : b * members_all + m + 1, :]
            w = jnp.concatenate([w] * (lats // 128), axis=1)
            coef = w * modes[b] if coef is None else coef + w * modes[b]
        increment = increment + coef * (level[m // mem_dev, m % mem_dev] - centre)
    analysis[me_mem] = centre + increment * norm
    piece = analysis.at[me_mem]
    fields = [
        send(piece, piece, field_send.at[d], field_recv.at[d], peer)
        for d, peer in enumerate(others)
    ]
    for copy in fields:
        copy.wait_recv()
    to_left.wait_send()
    to_right.wait_send()
    for copy in copies + shares + parts + spread + fields:
        copy.wait_send()


def unpack(system, work, size):
    lane = lax.broadcasted_iota(jnp.int32, (32, 128), 1)
    unit = jnp.where(
        lax.broadcasted_iota(jnp.int32, (128, 128), 0) == lax.broadcasted_iota(jnp.int32, (128, 128), 1),
        1.0, 0.0,
    )
    groups = system.shape[0]

    def take(t):
        return jnp.concatenate([system[g, t] for g in range(groups)], axis=0)

    last = [pltpu.roll(take(6), 64, 1), take(7)]
    thirds = [take(6), last[0], last[1]]
    for pair, (a, e) in enumerate(PAIRS):
        first, second, third = take(pair), take(3 + pair), thirds[pair]
        first_32, first_64, first_96 = (pltpu.roll(first, s, 1) for s in (96, 64, 32))
        second_32, second_64 = (pltpu.roll(second, s, 1) for s in (96, 64))
        third_32 = pltpu.roll(third, 96, 1)
        whole = jnp.concatenate(
            [
                first,
                jnp.where(lane < 32, first_32, second),
                jnp.where(lane < 32, first_64, jnp.where(lane < 64, second_32, third)),
                jnp.where(
                    lane < 32, first_96,
                    jnp.where(lane < 64, second_64, jnp.where(lane < 96, third_32, second_32)),
                ),
            ],
            axis=0,
        )
        if a == e:
            work[a * 128 : (a + 1) * 128, a * 128 : (a + 1) * 128] = whole + unit
        else:
            work[a * 128 : (a + 1) * 128, e * 128 : (e + 1) * 128] = whole
            work[e * 128 : (e + 1) * 128, a * 128 : (a + 1) * 128] = whole
    side = system[0, 7]
    turned = pltpu.roll(side, 64, 1)
    narrow = lax.broadcasted_iota(jnp.int32, (1, 128), 1)
    for a in range(KV):
        line = jnp.where(narrow < 64, side[a : a + 1], turned[KV + a : KV + a + 1])
        work[a * 128 : (a + 1) * 128, size : size + 128] = jnp.broadcast_to(line, (128, 128)).T


def row_of(x, j):
    return jnp.broadcast_to(x[j : j + 1, :], (8, 128))


def lanes_of(x, start):
    return [jnp.broadcast_to(x[:, start + c : start + c + 1], (8, 128)) for c in range(8)]


def added(terms):
    while len(terms) > 1:
        terms = [x + y for x, y in zip(terms[::2], terms[1::2])] + terms[len(terms) // 2 * 2 :]
    return terms[0]


def three_terms(x):
    high = x.astype(jnp.bfloat16)
    rest = x - high.astype(jnp.float32)
    middle = rest.astype(jnp.bfloat16)
    return high, middle, (rest - middle.astype(jnp.float32)).astype(jnp.bfloat16)


def wide_product(x, y):
    copies = x.shape[1] // y.shape[0]
    x0, x1, x2 = three_terms(x)
    y0, y1, y2 = three_terms(y)
    stack = [t for t in (y0, y0, y1, y1, y2, y0) for _ in range(copies)]
    return jnp.dot(
        jnp.concatenate([x0, x1, x0, x1, x0, x2], axis=1), jnp.concatenate(stack, axis=0),
        preferred_element_type=jnp.float32,
    )


def packed_product(x, y, shift):
    depth = y.shape[0]
    parts = 128 // depth
    part = lax.broadcasted_iota(jnp.int32, x.shape, 1) // depth
    own = x
    for k in range(1, parts):
        x = jnp.where(part == (shift // depth + k) % parts, pltpu.roll(own, k * depth, 1), x)
    x0, x1, x2 = (t.astype(jnp.float32) for t in three_terms(x))
    y0, y1, y2 = three_terms(y)
    pairs = [(x0, y0), (x1, y0), (x0, y1), (x1, y1), (x0, y2), (x2, y0)]
    pairs += [(jnp.zeros_like(x0), y0)] * (-len(pairs) % parts)
    left, right = [], []
    for at in range(0, len(pairs), parts):
        tile = pairs[at][0]
        for k in range(1, parts):
            tile = jnp.where(part == k, pairs[at + k][0], tile)
        left.append(tile.astype(jnp.bfloat16))
        right += [t for _, t in pairs[at : at + parts]]
    return jnp.dot(
        jnp.concatenate(left, axis=1), jnp.concatenate(right, axis=0),
        preferred_element_type=jnp.float32,
    )


def eliminate(work, size, columns):
    depth = 64
    blocks = depth // 8
    sub = lax.broadcasted_iota(jnp.int32, (8, 128), 0)
    lanes = lax.broadcasted_iota(jnp.int32, (8, 128), 1)
    for top in range(0, size, depth):
        low = top // 128 * 128
        shift = top - low
        mirror = (shift + 64) % 128
        inside = (lanes >= shift) & (lanes < shift + depth)
        panel = [
            jnp.where(
                inside, work[top + i * 8 : top + i * 8 + 8, low : low + 128],
                jnp.where(lanes - mirror == sub + i * 8, 1.0, 0.0),
            )
            for i in range(blocks)
        ]
        lead = lanes_of(panel[0], shift)
        for s in range(blocks):
            lane = shift + s * 8
            row = panel[s]
            ahead, corner, slope = [], [], []
            if s + 1 < blocks:
                ahead = lanes_of(row, lane + 8)
                corner = lanes_of(panel[s + 1], lane + 8)
                slope = lanes_of(panel[s + 1], lane)
            near = list(slope)
            scale = None
            for j in range(8):
                inv = 1.0 / row_of(lead[j], j)
                g = jnp.where(sub == j, 0.0, lead[j] * inv)
                h = slope[j] * inv if slope else None
                for c in range(j + 1, 8):
                    r = row_of(lead[c], j)
                    lead[c] = lead[c] - g * r
                    if slope:
                        slope[c] = slope[c] - h * r
                for c in range(len(ahead)):
                    r = row_of(ahead[c], j)
                    ahead[c] = ahead[c] - g * r
                    corner[c] = corner[c] - h * r
                row = row - g * row_of(row, j)
                scale = inv if scale is None else jnp.where(sub == j, inv, scale)
            lead = corner
            row = row * scale
            panel[s] = row
            spread = [row_of(row, j) for j in range(8)]
            for d in range(1, blocks):
                i = (s + d) % blocks
                factor = near if d == 1 and near else lanes_of(panel[i], lane)
                panel[i] = panel[i] - added([factor[j] * spread[j] for j in range(8)])
        image = (lanes >= mirror) & (lanes < mirror + depth)
        inverse = jnp.concatenate([jnp.where(image, x, 0.0) for x in panel], axis=0)
        first = (top + depth) // 128 * 128
        own = wide_product(inverse, work[top : top + depth, first:columns])
        others = [x for x in ((0, top), (top + depth, size)) if x[0] < x[1]]
        factor = jnp.concatenate([work[x:y, low : low + 128] for x, y in others], axis=0)
        change = packed_product(factor, own, shift)
        work[top : top + depth, first:columns] = own
        at = 0
        for x, y in others:
            work[x:y, first:columns] -= change[at : at + y - x]
            at += y - x


def store_kernel(prior, analysis, prior_out, analysis_out, sems):
    layers = prior.shape[0]
    copies = [bring(prior.at[l], prior_out.at[:, l], sems.at[l]) for l in range(layers)]
    copies.append(bring(analysis, analysis_out, sems.at[layers]))
    for copy in copies:
        copy.wait()


def params(collective=None):
    if collective is None:
        return pltpu.CompilerParams(vmem_limit_bytes=VMEM_LIMIT)
    return pltpu.CompilerParams(
        vmem_limit_bytes=VMEM_LIMIT, collective_id=collective, has_side_effects=True
    )


def fast_device(
    members, courant_lon, courant_lat, vert_modes, horiz_modes,
    obs_index, obs_count, obs_value, obs_var,
):
    f32 = jnp.float32
    bf16 = jnp.bfloat16
    mem_dev, layers, width, lats = members.shape
    n_lon = lax.axis_size("lon")
    n_mem = lax.axis_size("mem")
    total = mem_dev * n_mem
    size = total * MODES
    norm = (total - 1) ** (-0.5)
    slots = obs_index.shape[0]
    stack = mem_dev * layers
    index = obs_index.reshape(1, slots)
    dma = pltpu.SemaphoreType.DMA
    edge_rows = 2 * stack + 2 * layers
    prior, analysis = pl.pallas_call(
        functools.partial(front_kernel, n_lon, n_mem, norm),
        out_shape=(
            jax.ShapeDtypeStruct((layers, mem_dev, width, lats), f32),
            jax.ShapeDtypeStruct((layers, width, lats), f32),
        ),
        in_specs=[hbm()] * 8 + [smem()],
        out_specs=(vmem(),) * 2,
        scratch_shapes=[
            pltpu.VMEM((n_mem, mem_dev, width, lats), f32),
            pltpu.VMEM((n_mem, n_lon, 8, 128), f32),
            pltpu.VMEM((size, size + 128), f32),
            pltpu.VMEM((stack, width + 8, lats), f32),
            pltpu.VMEM((layers, width + 8, lats), f32),
            pltpu.VMEM((layers, width + 8, lats), f32),
            pltpu.VMEM((KH, width, lats), f32),
            pltpu.VMEM((1, slots), jnp.int32),
            pltpu.VMEM((1, slots), f32),
            pltpu.VMEM((1, slots), f32),
            pltpu.VMEM((KV, layers), f32),
            pltpu.VMEM((2, edge_rows, lats), f32),
            pltpu.VMEM((2, edge_rows, lats), f32),
            pltpu.VMEM((2 * lats, slots), bf16),
            pltpu.VMEM((stack * width, 2 * lats), bf16),
            pltpu.VMEM((n_mem, mem_dev, slots), f32),
            pltpu.VMEM((8, slots), f32),
            pltpu.VMEM((3 * KH * mem_dev + 16, 128), f32),
            pltpu.VMEM((n_lon, 8, 128), f32),
            pltpu.VMEM((n_lon, 8, 128), f32),
            dma((mem_dev + 7,)),
            dma((2,)), dma((2,)),
            dma((GROUPS, n_mem - 1)), dma((GROUPS, n_mem - 1)),
            pltpu.SemaphoreType.REGULAR,
            dma((n_lon - 1,)), dma((n_lon - 1,)),
            dma((n_lon * n_mem,)), dma((n_lon * n_mem,)),
            dma((n_mem - 1,)), dma((n_mem - 1,)),
            dma((n_mem - 1,)), dma((n_mem - 1,)),
        ],
        compiler_params=params(1),
        name="front",
    )(
        *map(
            stay,
            (
                members, courant_lon, courant_lat, horiz_modes, index,
                obs_value.reshape(1, slots), obs_var.reshape(1, slots), vert_modes,
            ),
        ),
        obs_count,
    )
    return pl.pallas_call(
        store_kernel,
        out_shape=(
            jax.ShapeDtypeStruct((mem_dev, layers, width, lats), f32),
            jax.ShapeDtypeStruct((layers, width, lats), f32),
        ),
        in_specs=[vmem()] * 2,
        out_specs=(hbm(), hbm()),
        scratch_shapes=[dma((layers + 1,))],
        compiler_params=params(),
        name="store",
    )(prior, analysis)


def padded(block, sides, width):
    for axis, dim in sides:
        count = lax.axis_size(axis)
        forward = [(i, i + 1) for i in range(count - 1)]
        forward.append((count - 1, 0))
        backward = [(target, source) for source, target in forward]
        low = lax.ppermute(
            lax.slice_in_dim(block, block.shape[dim] - width, None, axis=dim), axis, forward
        )
        high = lax.ppermute(lax.slice_in_dim(block, 0, width, axis=dim), axis, backward)
        block = jnp.concatenate([low, block, high], axis=dim)
    return block


def update(centre, western, eastern, flow_lon, flow_lat):
    zero_col = jnp.zeros_like(centre[..., :1])
    south_boundary = jnp.concatenate([zero_col, centre[..., :-1]], axis=-1)
    northern = jnp.concatenate([centre[..., 1:], zero_col], axis=-1)
    result = centre - jnp.maximum(flow_lon, 0.0) * (centre - western)
    result = result - jnp.minimum(flow_lon, 0.0) * (eastern - centre)
    result = result - jnp.maximum(flow_lat, 0.0) * (centre - south_boundary)
    result = result - jnp.minimum(flow_lat, 0.0) * (northern - centre)
    return result


def per_device(
    members,
    courant_lon,
    courant_lat,
    vert_modes,
    horiz_modes,
    obs_index,
    obs_count,
    obs_value,
    obs_var,
):
    mem_dev, layer_tally, band_width, lat_rows = members.shape
    sample_tally_overall = mem_dev * lax.axis_size("mem")
    rim_depth = ADV_STEPS
    stacked = jnp.concatenate(
        [members.reshape(mem_dev * layer_tally, band_width, lat_rows), courant_lon, courant_lat],
        axis=0,
    )
    extended = padded(stacked, (("lon", 1),), rim_depth)
    split_at = mem_dev * layer_tally
    prognostic_vector = extended[:split_at].reshape(
        mem_dev, layer_tally, band_width + 2 * rim_depth, lat_rows
    )
    flow_lon_ext = extended[split_at : split_at + layer_tally]
    meridional_wind_padded = extended[split_at + layer_tally :]
    for section in range(rim_depth):
        out_cols = band_width + 2 * (rim_depth - 1 - section)
        first_col = section + 1
        prognostic_vector = update(
            prognostic_vector[:, :, 1 : out_cols + 1],
            prognostic_vector[:, :, 0:out_cols],
            prognostic_vector[:, :, 2 : out_cols + 2],
            flow_lon_ext[:, first_col : first_col + out_cols],
            meridional_wind_padded[:, first_col : first_col + out_cols],
        )
    sample_centroid = lax.psum(jnp.sum(prognostic_vector, axis=0), "mem") / sample_tally_overall
    sample_departure = prognostic_vector - sample_centroid[None]
    norm_scale = (sample_tally_overall - 1) ** (-0.5)
    obs_slots = obs_index.shape[0]
    band_cells = band_width * lat_rows
    level_idx = obs_index // band_cells
    within = obs_index % band_cells
    anomaly_obs = jnp.take(sample_departure.reshape(mem_dev, -1), obs_index, axis=1)
    mean_obs = jnp.take(sample_centroid.reshape(-1), obs_index)
    vert_obs = jnp.take(vert_modes, level_idx, axis=1)
    horiz_obs = jnp.take(horiz_modes.reshape(KH, -1), within, axis=1)
    modes_obs = (vert_obs[:, None, :] * horiz_obs[None, :, :]).reshape(KV * KH, obs_slots)
    live_mask = (jnp.arange(obs_slots, dtype=jnp.int32) < obs_count[0]).astype(jnp.float32)
    obs_perts = (
        anomaly_obs[:, None, :] * modes_obs[None, :, :] * (live_mask * norm_scale)[None, None, :]
    )
    obs_perts = obs_perts.reshape(mem_dev * KV * KH, obs_slots)
    inv_var = live_mask / obs_var
    innovation = obs_value - mean_obs
    all_perts = lax.all_gather(obs_perts, "mem", axis=0, tiled=True)
    gram_part = jnp.dot(all_perts * inv_var[None, :], all_perts.T, precision=lax.Precision.HIGHEST)
    side_part = jnp.dot(all_perts, inv_var * innovation, precision=lax.Precision.HIGHEST)
    gram_matrix, right_side = lax.psum((gram_part, side_part), "lon")
    system = jnp.eye(gram_matrix.shape[0], dtype=jnp.float32) + gram_matrix
    factor = jnp.linalg.cholesky(system)
    weights = jax.scipy.linalg.cho_solve((factor, True), right_side)
    w_mat = weights.reshape(sample_tally_overall, KV * KH)
    w_local = lax.dynamic_slice_in_dim(w_mat, lax.axis_index("mem") * mem_dev, mem_dev, 0)
    mode_coef = jnp.einsum(
        "mk,mlij->klij", w_local, sample_departure, precision=lax.Precision.HIGHEST
    )
    mode_coef = mode_coef.reshape(KV, KH, layer_tally, band_width, lat_rows)
    inc_part = (
        jnp.einsum(
            "al,bij,ablij->lij", vert_modes, horiz_modes, mode_coef, precision=lax.Precision.HIGHEST
        )
        * norm_scale
    )
    posterior_adjustment = lax.psum(inc_part, "mem")
    return (prognostic_vector, sample_centroid + posterior_adjustment)


def choose(*args):
    mem_dev, layers, width, lats = args[0].shape
    n_lon = lax.axis_size("lon")
    n_mem = lax.axis_size("mem")
    fits = (
        mem_dev == 8
        and layers == 4
        and n_mem == layers
        and n_lon == 8
        and width % 8 == 0
        and lats == 256
        and args[5].shape[0] % (GROUPS * PIECE) == 0
    )
    return fast_device(*args) if fits else per_device(*args)


def solution(mesh):
    placed = (
        P("mem", None, "lon", None),
        P(None, "lon", None),
        P(None, "lon", None),
        P(),
        P(None, "lon", None),
        P("lon"),
        P("lon"),
        P("lon"),
        P("lon"),
    )
    return jax.shard_map(
        choose,
        mesh=mesh,
        in_specs=placed,
        out_specs=(P("mem", None, "lon", None), P(None, "lon", None)),
        check_vma=False,
    )
```

```python
import functools

import jax
import jax.numpy as jnp
from jax import lax
from jax.experimental import pallas as pl
from jax.experimental.pallas import tpu as pltpu
from jax.sharding import PartitionSpec as P

KV = 2
KH = 4
ADV_STEPS = 2
MODES = KV * KH
PAIRS = ((0, 0), (0, 1), (1, 1))
MESH = pl.DeviceIdType.MESH
VMEM_LIMIT = 24 * 1024 * 1024
HIGHEST = lax.Precision.HIGHEST
PIECE = 512
GROUPS = 4


def vmem():
    return pl.BlockSpec(memory_space=pltpu.VMEM)


def smem():
    return pl.BlockSpec(memory_space=pltpu.SMEM)


def hbm():
    return pl.BlockSpec(memory_space=pltpu.HBM)


def stay(x):
    return pltpu.with_memory_space_constraint(x, pltpu.HBM)


def greet(peers):
    barrier = pltpu.get_barrier_semaphore()
    for peer in peers:
        pl.semaphore_signal(barrier, inc=1, device_id=peer, device_id_type=MESH)
    return barrier


def axis_peers(axis, count):
    me = lax.axis_index(axis)
    return [{axis: lax.rem(me + d, count)} for d in range(1, count)]


def send(src, dst, send_sem, recv_sem, peer):
    copy = pltpu.make_async_remote_copy(
        src_ref=src, dst_ref=dst, send_sem=send_sem, recv_sem=recv_sem,
        device_id=peer, device_id_type=MESH,
    )
    copy.start()
    return copy


def bring(src, dst, sem):
    copy = pltpu.make_async_copy(src, dst, sem)
    copy.start()
    return copy


def two_terms(x):
    high = x.astype(jnp.bfloat16)
    return high, (x - high.astype(jnp.float32)).astype(jnp.bfloat16)


def front_kernel(
    n_lon, n_mem, norm,
    members, cx, cy, horiz, index, value_in, var_in, vert_in, count,
    prior, analysis,
    level, system, work, ext, cx_ext, cy_ext, modes, cells, value, var, vert, edge_out, edge_in, spots, terms, gathered,
    obs_horiz, total, staged, heard,
    in_sem, edge_send, edge_recv, obs_send, obs_recv, far_sem,
    part_send, part_recv, all_send, all_recv, level_send, level_recv, field_send, field_recv,
):
    mem_dev, layers, width, lats = members.shape
    stack = mem_dev * layers
    slots = index.shape[1]
    tiles = width // 8
    shift = lats.bit_length() - 1
    me = lax.axis_index("lon")
    me_mem = lax.axis_index("mem")
    left = {"lon": lax.rem(me + n_lon - 1, n_lon)}
    right = {"lon": lax.rem(me + 1, n_lon)}
    others = axis_peers("mem", n_mem)

    states = [
        bring(members.at[m], ext.at[pl.ds(m * layers, layers), pl.ds(0, width), :], in_sem.at[m])
        for m in range(mem_dev)
    ]
    flows = [
        bring(cx, cx_ext.at[:, pl.ds(0, width), :], in_sem.at[mem_dev]),
        bring(cy, cy_ext.at[:, pl.ds(0, width), :], in_sem.at[mem_dev + 1]),
    ]
    places = bring(index, cells, in_sem.at[mem_dev + 2])
    shapes = bring(horiz, modes, in_sem.at[mem_dev + 3])
    observed = [
        bring(src, dst, in_sem.at[mem_dev + 4 + i])
        for i, (src, dst) in enumerate(((value_in, value), (var_in, var), (vert_in, vert)))
    ]
    barrier = greet([left, right] + others)
    for copy in states + flows:
        copy.wait()
    for side, (first, second, rim) in enumerate(((0, 1, 0), (width - 2, width - 1, width - 1))):
        edge_out[side, 0:stack, :] = ext[:, first, :]
        edge_out[side, stack : 2 * stack, :] = ext[:, second, :]
        edge_out[side, 2 * stack : 2 * stack + layers, :] = cx_ext[:, rim, :]
        edge_out[side, 2 * stack + layers : 2 * stack + 2 * layers, :] = cy_ext[:, rim, :]
    pl.semaphore_wait(barrier, 2 + len(others))
    to_left = send(edge_out.at[0], edge_in.at[1], edge_send.at[0], edge_recv.at[1], left)
    to_right = send(edge_out.at[1], edge_in.at[0], edge_send.at[1], edge_recv.at[0], right)

    places.wait()
    shapes.wait()
    sub = lax.broadcasted_iota(jnp.int32, (8, 128), 0)
    lat_row = lax.broadcasted_iota(jnp.int32, (lats, PIECE), 0)

    def rows_of(start):
        return jnp.broadcast_to(lax.shift_right_logical(cells[:, pl.ds(start, 128)], shift), (8, 128))

    def picked(found, tile, wanted, blocks, origin):
        total = [jnp.zeros((8, 128), jnp.float32)] * blocks
        for t, rows in wanted:
            here = tile == t
            total = [
                jnp.where(here, found[rows + origin(k) : rows + origin(k) + 8], x)
                for k, x in enumerate(total)
            ]
        return total

    def settle(values, sublane):
        here = sub == sublane
        sums = [jnp.sum(jnp.where(here, x, 0.0), axis=0, keepdims=True) for x in values]
        while len(sums) < 8:
            sums.append(jnp.zeros((1, 128), jnp.float32))
        return jnp.concatenate(sums, axis=0)

    mode_terms = jnp.concatenate(two_terms(modes[...].reshape(KH * width, lats)), axis=1)

    def spot(c, carry):
        start = pl.multiple_of(c * PIECE, PIECE)
        lat = jnp.bitwise_and(cells[:, pl.ds(start, PIECE)], lats - 1)
        mask = jnp.where(lat_row == lat, 1.0, 0.0).astype(jnp.bfloat16)
        spots[0:lats, pl.ds(start, PIECE)] = mask
        spots[lats : 2 * lats, pl.ds(start, PIECE)] = mask
        found = jnp.dot(
            mode_terms, jnp.concatenate([mask, mask], axis=0), preferred_element_type=jnp.float32
        )
        for h in range(PIECE // 128):
            low = pl.multiple_of(start + h * 128, 128)
            row = rows_of(low)
            for l in range(1, layers):
                row = jnp.where(rows_of(low) >= l * width, rows_of(low) - l * width, row)
            tile = lax.shift_right_logical(row, 3)
            part = found[:, h * 128 : (h + 1) * 128]
            values = picked(part, tile, [(t, t * 8) for t in range(tiles)], KH, lambda k: k * width)
            obs_horiz[:, pl.ds(low, 128)] = settle(values, jnp.bitwise_and(row, 7))
        return carry

    lax.fori_loop(0, slots // PIECE, spot, 0)

    to_left.wait_recv()
    to_right.wait_recv()
    for d in (2, n_lon - 2):
        pl.semaphore_signal(
            far_sem, inc=1, device_id={"lon": lax.rem(me + d, n_lon)}, device_id_type=MESH
        )
    ext_rows = width + 8
    last = ext_rows - 1
    ext[:, last - 1, :] = edge_in[0, 0:stack, :]
    ext[:, last, :] = edge_in[0, stack : 2 * stack, :]
    ext[:, width, :] = edge_in[1, 0:stack, :]
    ext[:, width + 1, :] = edge_in[1, stack : 2 * stack, :]
    for side, row in ((0, last), (1, width)):
        cx_ext[:, row, :] = edge_in[side, 2 * stack : 2 * stack + layers, :]
        cy_ext[:, row, :] = edge_in[side, 2 * stack + layers : 2 * stack + 2 * layers, :]

    lane = lax.broadcasted_iota(jnp.int32, (ext_rows, lats), 1)
    for l in range(layers):
        cx_l = cx_ext[l]
        cy_l = cy_ext[l]
        east_flow = jnp.maximum(cx_l, 0.0)
        west_flow = jnp.minimum(cx_l, 0.0)
        north_flow = jnp.maximum(cy_l, 0.0)
        south_flow = jnp.minimum(cy_l, 0.0)

        def step(pair, carry, l=l, flows=(east_flow, west_flow, north_flow, south_flow)):
            inner = []
            for k in range(2):
                m = pair * 2 + k
                q = ext[m * layers + l]
                for _ in range(ADV_STEPS):
                    qw = pltpu.roll(q, 1, 0)
                    qe = pltpu.roll(q, ext_rows - 1, 0)
                    qs = jnp.where(lane == 0, 0.0, pltpu.roll(q, 1, 1))
                    qn = jnp.where(lane == lats - 1, 0.0, pltpu.roll(q, lats - 1, 1))
                    r = q - flows[0] * (q - qw)
                    r = r - flows[1] * (qe - q)
                    r = r - flows[2] * (q - qs)
                    q = r - flows[3] * (qn - q)
                inner.append(q[0:width, :])
                prior[l, m] = q[0:width, :]
            start = pl.multiple_of((l * mem_dev + pair * 2) * width, 16)
            high, low = two_terms(jnp.concatenate(inner, axis=0))
            terms[pl.ds(start, 2 * width), 0:lats] = high
            terms[pl.ds(start, 2 * width), lats : 2 * lats] = low
            return carry

        lax.fori_loop(0, mem_dev // 2, step, 0, unroll=2)

    wanted = [(l * tiles + t, l * mem_dev * width + t * 8) for l in range(layers) for t in range(tiles)]

    def gather(c, carry):
        start = pl.multiple_of(c * PIECE, PIECE)
        found = jnp.dot(
            terms[...], spots[:, pl.ds(start, PIECE)], preferred_element_type=jnp.float32
        )
        for h in range(PIECE // 128):
            low = pl.multiple_of(start + h * 128, 128)
            row = rows_of(low)
            part = found[:, h * 128 : (h + 1) * 128]
            tile = lax.shift_right_logical(row, 3)
            values = picked(part, tile, wanted, mem_dev, lambda k: k * width)
            gathered[me_mem, :, pl.ds(low, 128)] = settle(values, jnp.bitwise_and(row, 7))
        return carry

    span = slots // GROUPS
    steps = span // PIECE
    copies = []
    for c in range(GROUPS):
        lax.fori_loop(c * steps, (c + 1) * steps, gather, 0)
        piece = gathered.at[me_mem, :, pl.ds(c * span, span)]
        for d, peer in enumerate(others):
            copies.append(send(piece, piece, obs_send.at[c, d], obs_recv.at[c, d], peer))
    early = 4
    shares = [
        send(
            prior.at[peer["mem"], pl.ds(0, early)], level.at[me_mem, pl.ds(0, early)],
            level_send.at[0, d], level_recv.at[0, d], peer,
        )
        for d, peer in enumerate(others)
    ]
    level[me_mem] = prior[me_mem]

    members_all = n_mem * mem_dev
    for copy in observed:
        copy.wait()
    slot = lax.broadcasted_iota(jnp.int32, (1, span), 1)
    head = lax.broadcasted_iota(jnp.int32, (8, span), 0)
    factors = [[jnp.broadcast_to(vert[a : a + 1, l : l + 1], (1, span)) for l in range(layers)] for a in range(KV)]
    contract = (((1,), (1,)), ((), ()))

    def part(c):
        at = pl.ds(c * span, span)
        states = gathered[:, :, at].reshape(members_all, span)
        centre = jnp.sum(states, axis=0, keepdims=True) / members_all
        anomaly = states - centre
        mine = gathered[me_mem, :, at] - centre
        cell = cells[:, at]
        v = []
        for a in range(KV):
            x = factors[a][0]
            for l in range(1, layers):
                x = jnp.where(cell >= l * width * lats, factors[a][l], x)
            v.append(x)
        inv_var = jnp.where(slot + c * span < count[0], 1.0, 0.0) / var[:, at]
        drive = inv_var * (value[:, at] - centre) * norm
        weight = inv_var * (norm * norm)
        local_modes = obs_horiz[0:KH, at]
        wide = jnp.concatenate([anomaly * local_modes[b : b + 1] for b in range(KH)], axis=0)
        own = jnp.concatenate([mine * local_modes[b : b + 1] for b in range(KH)], axis=0)
        drives = jnp.where(head == 0, v[0] * drive, jnp.where(head == 1, v[1] * drive, 0.0))
        narrow = jnp.concatenate(
            [own * (v[a] * v[e] * weight) for a, e in PAIRS] + [drives, jnp.zeros_like(drives)], axis=0
        )
        wide_high, wide_low = two_terms(wide)
        narrow_high, narrow_low = two_terms(narrow)
        first = lax.dot_general(
            jnp.concatenate([narrow_high, narrow_low], axis=0), wide_high, contract,
            preferred_element_type=jnp.float32,
        )
        second = lax.dot_general(
            narrow_high, wide_low, contract, preferred_element_type=jnp.float32
        )
        rows = narrow.shape[0]
        return first[0:rows] + first[rows : 2 * rows] + second

    peers = len(others)
    for c in range(GROUPS):
        for copy in copies[c * peers : (c + 1) * peers]:
            copy.wait_recv()
        if c == 0:
            total[...] = part(c)
        else:
            total[...] += part(c)
    local = KH * mem_dev
    lane = lax.broadcasted_iota(jnp.int32, (8, 128), 1)

    def block(pair, b):
        return total[pair * local + b * 8 : pair * local + b * 8 + 8, :]

    for pair in range(3):
        staged[pair] = block(pair, 0)
        staged[3 + pair] = jnp.where(lane < 32, pltpu.roll(block(pair, 3), 32, 1), block(pair, 1))
    staged[6] = jnp.where(lane < 64, pltpu.roll(block(1, 2), 64, 1), block(0, 2))
    side = total[3 * local : 3 * local + 8, :]
    other = pltpu.roll(pltpu.roll(side, 64, 1), KV, 0)
    staged[7] = jnp.where(lane < 64, jnp.where(sub < KV, side, other), block(2, 2))

    pl.semaphore_wait(far_sem, 2)
    parts = [
        send(staged.at[peer["lon"]], heard.at[me], part_send.at[d], part_recv.at[d], peer)
        for d, peer in enumerate(axis_peers("lon", n_lon))
    ]
    heard[me] = staged[me]
    for copy in parts:
        copy.wait_recv()
    summed = heard[0]
    for d in range(1, n_lon):
        summed = summed + heard[d]
    core, row = lax.rem(me, 2), lax.div(me, 2)
    system[core, me_mem, row] = summed
    piece = system.at[core, me_mem, row]
    spread = []
    for hop in range(1, n_lon // 2 * n_mem):
        peer = {
            "lon": lax.rem(me + hop // n_mem * 2, n_lon),
            "mem": lax.rem(me_mem + hop % n_mem, n_mem),
        }
        spread.append(send(piece, piece, all_send.at[hop], all_recv.at[hop], peer))
    for copy in spread:
        copy.wait_recv()
    half = system.at[core]
    spread.append(send(half, half, all_send.at[0], all_recv.at[0], {"lon": me + 1 - 2 * core}))
    spread[-1].wait_recv()

    shares += [
        send(
            prior.at[peer["mem"], pl.ds(early, mem_dev - early)], level.at[me_mem, pl.ds(early, mem_dev - early)],
            level_send.at[1, d], level_recv.at[1, d], peer,
        )
        for d, peer in enumerate(others)
    ]
    size = members_all * MODES
    columns = size + 128
    unpack(system, work, size)
    eliminate(work, size, columns)
    half = size // KV
    lines = []
    for a in range(KV):
        x = jnp.broadcast_to(vert[a : a + 1, 0:1], (1, 128))
        for l in range(1, layers):
            x = jnp.where(me_mem == l, jnp.broadcast_to(vert[a : a + 1, l : l + 1], (1, 128)), x)
        lines.append(x)
    mixed = lines[0] * work[0:half, size:columns] + lines[1] * work[half:size, size:columns]
    for copy in shares:
        copy.wait_recv()
    centre = level[0, 0]
    for m in range(1, members_all):
        centre = centre + level[m // mem_dev, m % mem_dev]
    centre = centre / members_all
    increment = jnp.zeros_like(centre)
    for m in range(members_all):
        coef = None
        for b in range(KH):
            w = mixed[b * members_all + m : b * members_all + m + 1, :]
            w = jnp.concatenate([w] * (lats // 128), axis=1)
            coef = w * modes[b] if coef is None else coef + w * modes[b]
        increment = increment + coef * (level[m // mem_dev, m % mem_dev] - centre)
    analysis[me_mem] = centre + increment * norm
    piece = analysis.at[me_mem]
    fields = [
        send(piece, piece, field_send.at[d], field_recv.at[d], peer)
        for d, peer in enumerate(others)
    ]
    for copy in fields:
        copy.wait_recv()
    to_left.wait_send()
    to_right.wait_send()
    for copy in copies + shares + parts + spread + fields:
        copy.wait_send()


def unpack(system, work, size):
    lane = lax.broadcasted_iota(jnp.int32, (32, 128), 1)
    unit = jnp.where(
        lax.broadcasted_iota(jnp.int32, (128, 128), 0) == lax.broadcasted_iota(jnp.int32, (128, 128), 1),
        1.0, 0.0,
    )
    groups = system.shape[1]

    def take(t):
        return jnp.concatenate([system[t % 2, g, t // 2] for g in range(groups)], axis=0)

    last = [pltpu.roll(take(6), 64, 1), take(7)]
    thirds = [take(6), last[0], last[1]]
    for pair, (a, e) in enumerate(PAIRS):
        first, second, third = take(pair), take(3 + pair), thirds[pair]
        first_32, first_64, first_96 = (pltpu.roll(first, s, 1) for s in (96, 64, 32))
        second_32, second_64 = (pltpu.roll(second, s, 1) for s in (96, 64))
        third_32 = pltpu.roll(third, 96, 1)
        whole = jnp.concatenate(
            [
                first,
                jnp.where(lane < 32, first_32, second),
                jnp.where(lane < 32, first_64, jnp.where(lane < 64, second_32, third)),
                jnp.where(
                    lane < 32, first_96,
                    jnp.where(lane < 64, second_64, jnp.where(lane < 96, third_32, second_32)),
                ),
            ],
            axis=0,
        )
        if a == e:
            work[a * 128 : (a + 1) * 128, a * 128 : (a + 1) * 128] = whole + unit
        else:
            work[a * 128 : (a + 1) * 128, e * 128 : (e + 1) * 128] = whole
            work[e * 128 : (e + 1) * 128, a * 128 : (a + 1) * 128] = whole
    side = system[1, 0, 3]
    turned = pltpu.roll(side, 64, 1)
    narrow = lax.broadcasted_iota(jnp.int32, (1, 128), 1)
    for a in range(KV):
        line = jnp.where(narrow < 64, side[a : a + 1], turned[KV + a : KV + a + 1])
        work[a * 128 : (a + 1) * 128, size : size + 128] = jnp.broadcast_to(line, (128, 128)).T


def row_of(x, j):
    return jnp.broadcast_to(x[j : j + 1, :], (8, 128))


def lanes_of(x, start):
    return [jnp.broadcast_to(x[:, start + c : start + c + 1], (8, 128)) for c in range(8)]


def added(terms):
    while len(terms) > 1:
        terms = [x + y for x, y in zip(terms[::2], terms[1::2])] + terms[len(terms) // 2 * 2 :]
    return terms[0]


def three_terms(x):
    high = x.astype(jnp.bfloat16)
    rest = x - high.astype(jnp.float32)
    middle = rest.astype(jnp.bfloat16)
    return high, middle, (rest - middle.astype(jnp.float32)).astype(jnp.bfloat16)


def wide_product(x, y):
    copies = x.shape[1] // y.shape[0]
    x0, x1, x2 = three_terms(x)
    y0, y1, y2 = three_terms(y)
    stack = [t for t in (y0, y0, y1, y1, y2, y0) for _ in range(copies)]
    return jnp.dot(
        jnp.concatenate([x0, x1, x0, x1, x0, x2], axis=1), jnp.concatenate(stack, axis=0),
        preferred_element_type=jnp.float32,
    )


def packed_product(x, y, shift):
    depth = y.shape[0]
    parts = 128 // depth
    part = lax.broadcasted_iota(jnp.int32, x.shape, 1) // depth
    own = x
    for k in range(1, parts):
        x = jnp.where(part == (shift // depth + k) % parts, pltpu.roll(own, k * depth, 1), x)
    x0, x1, x2 = (t.astype(jnp.float32) for t in three_terms(x))
    y0, y1, y2 = three_terms(y)
    pairs = [(x0, y0), (x1, y0), (x0, y1), (x1, y1), (x0, y2), (x2, y0)]
    pairs += [(jnp.zeros_like(x0), y0)] * (-len(pairs) % parts)
    left, right = [], []
    for at in range(0, len(pairs), parts):
        tile = pairs[at][0]
        for k in range(1, parts):
            tile = jnp.where(part == k, pairs[at + k][0], tile)
        left.append(tile.astype(jnp.bfloat16))
        right += [t for _, t in pairs[at : at + parts]]
    return jnp.dot(
        jnp.concatenate(left, axis=1), jnp.concatenate(right, axis=0),
        preferred_element_type=jnp.float32,
    )


def eliminate(work, size, columns):
    depth = 64
    blocks = depth // 8
    sub = lax.broadcasted_iota(jnp.int32, (8, 128), 0)
    lanes = lax.broadcasted_iota(jnp.int32, (8, 128), 1)
    for top in range(0, size, depth):
        low = top // 128 * 128
        shift = top - low
        mirror = (shift + 64) % 128
        inside = (lanes >= shift) & (lanes < shift + depth)
        panel = [
            jnp.where(
                inside, work[top + i * 8 : top + i * 8 + 8, low : low + 128],
                jnp.where(lanes - mirror == sub + i * 8, 1.0, 0.0),
            )
            for i in range(blocks)
        ]
        lead = lanes_of(panel[0], shift)
        for s in range(blocks):
            lane = shift + s * 8
            row = panel[s]
            ahead, corner, slope = [], [], []
            if s + 1 < blocks:
                ahead = lanes_of(row, lane + 8)
                corner = lanes_of(panel[s + 1], lane + 8)
                slope = lanes_of(panel[s + 1], lane)
            near = list(slope)
            scale = None
            for j in range(8):
                inv = 1.0 / row_of(lead[j], j)
                g = jnp.where(sub == j, 0.0, lead[j] * inv)
                h = slope[j] * inv if slope else None
                for c in range(j + 1, 8):
                    r = row_of(lead[c], j)
                    lead[c] = lead[c] - g * r
                    if slope:
                        slope[c] = slope[c] - h * r
                for c in range(len(ahead)):
                    r = row_of(ahead[c], j)
                    ahead[c] = ahead[c] - g * r
                    corner[c] = corner[c] - h * r
                row = row - g * row_of(row, j)
                scale = inv if scale is None else jnp.where(sub == j, inv, scale)
            lead = corner
            row = row * scale
            panel[s] = row
            spread = [row_of(row, j) for j in range(8)]
            for d in range(1, blocks):
                i = (s + d) % blocks
                factor = near if d == 1 and near else lanes_of(panel[i], lane)
                panel[i] = panel[i] - added([factor[j] * spread[j] for j in range(8)])
        image = (lanes >= mirror) & (lanes < mirror + depth)
        inverse = jnp.concatenate([jnp.where(image, x, 0.0) for x in panel], axis=0)
        first = (top + depth) // 128 * 128
        own = wide_product(inverse, work[top : top + depth, first:columns])
        others = [x for x in ((0, top), (top + depth, size)) if x[0] < x[1]]
        factor = jnp.concatenate([work[x:y, low : low + 128] for x, y in others], axis=0)
        change = packed_product(factor, own, shift)
        work[top : top + depth, first:columns] = own
        at = 0
        for x, y in others:
            work[x:y, first:columns] -= change[at : at + y - x]
            at += y - x


def store_kernel(prior, analysis, prior_out, analysis_out, sems):
    layers = prior.shape[0]
    copies = [bring(prior.at[l], prior_out.at[:, l], sems.at[l]) for l in range(layers)]
    copies.append(bring(analysis, analysis_out, sems.at[layers]))
    for copy in copies:
        copy.wait()


def params(collective=None):
    if collective is None:
        return pltpu.CompilerParams(vmem_limit_bytes=VMEM_LIMIT)
    return pltpu.CompilerParams(
        vmem_limit_bytes=VMEM_LIMIT, collective_id=collective, has_side_effects=True
    )


def fast_device(
    members, courant_lon, courant_lat, vert_modes, horiz_modes,
    obs_index, obs_count, obs_value, obs_var,
):
    f32 = jnp.float32
    bf16 = jnp.bfloat16
    mem_dev, layers, width, lats = members.shape
    n_lon = lax.axis_size("lon")
    n_mem = lax.axis_size("mem")
    total = mem_dev * n_mem
    size = total * MODES
    norm = (total - 1) ** (-0.5)
    slots = obs_index.shape[0]
    stack = mem_dev * layers
    index = obs_index.reshape(1, slots)
    dma = pltpu.SemaphoreType.DMA
    edge_rows = 2 * stack + 2 * layers
    prior, analysis = pl.pallas_call(
        functools.partial(front_kernel, n_lon, n_mem, norm),
        out_shape=(
            jax.ShapeDtypeStruct((layers, mem_dev, width, lats), f32),
            jax.ShapeDtypeStruct((layers, width, lats), f32),
        ),
        in_specs=[hbm()] * 8 + [smem()],
        out_specs=(vmem(),) * 2,
        scratch_shapes=[
            pltpu.VMEM((n_mem, mem_dev, width, lats), f32),
            pltpu.VMEM((2, n_mem, n_lon // 2, 8, 128), f32),
            pltpu.VMEM((size, size + 128), f32),
            pltpu.VMEM((stack, width + 8, lats), f32),
            pltpu.VMEM((layers, width + 8, lats), f32),
            pltpu.VMEM((layers, width + 8, lats), f32),
            pltpu.VMEM((KH, width, lats), f32),
            pltpu.VMEM((1, slots), jnp.int32),
            pltpu.VMEM((1, slots), f32),
            pltpu.VMEM((1, slots), f32),
            pltpu.VMEM((KV, layers), f32),
            pltpu.VMEM((2, edge_rows, lats), f32),
            pltpu.VMEM((2, edge_rows, lats), f32),
            pltpu.VMEM((2 * lats, slots), bf16),
            pltpu.VMEM((stack * width, 2 * lats), bf16),
            pltpu.VMEM((n_mem, mem_dev, slots), f32),
            pltpu.VMEM((8, slots), f32),
            pltpu.VMEM((3 * KH * mem_dev + 16, 128), f32),
            pltpu.VMEM((n_lon, 8, 128), f32),
            pltpu.VMEM((n_lon, 8, 128), f32),
            dma((mem_dev + 7,)),
            dma((2,)), dma((2,)),
            dma((GROUPS, n_mem - 1)), dma((GROUPS, n_mem - 1)),
            pltpu.SemaphoreType.REGULAR,
            dma((n_lon - 1,)), dma((n_lon - 1,)),
            dma((n_lon // 2 * n_mem,)), dma((n_lon // 2 * n_mem,)),
            dma((2, n_mem - 1)), dma((2, n_mem - 1)),
            dma((n_mem - 1,)), dma((n_mem - 1,)),
        ],
        compiler_params=params(1),
        name="front",
    )(
        *map(
            stay,
            (
                members, courant_lon, courant_lat, horiz_modes, index,
                obs_value.reshape(1, slots), obs_var.reshape(1, slots), vert_modes,
            ),
        ),
        obs_count,
    )
    return pl.pallas_call(
        store_kernel,
        out_shape=(
            jax.ShapeDtypeStruct((mem_dev, layers, width, lats), f32),
            jax.ShapeDtypeStruct((layers, width, lats), f32),
        ),
        in_specs=[vmem()] * 2,
        out_specs=(hbm(), hbm()),
        scratch_shapes=[dma((layers + 1,))],
        compiler_params=params(),
        name="store",
    )(prior, analysis)


def padded(block, sides, width):
    for axis, dim in sides:
        count = lax.axis_size(axis)
        forward = [(i, i + 1) for i in range(count - 1)]
        forward.append((count - 1, 0))
        backward = [(target, source) for source, target in forward]
        low = lax.ppermute(
            lax.slice_in_dim(block, block.shape[dim] - width, None, axis=dim), axis, forward
        )
        high = lax.ppermute(lax.slice_in_dim(block, 0, width, axis=dim), axis, backward)
        block = jnp.concatenate([low, block, high], axis=dim)
    return block


def update(centre, western, eastern, flow_lon, flow_lat):
    zero_col = jnp.zeros_like(centre[..., :1])
    south_boundary = jnp.concatenate([zero_col, centre[..., :-1]], axis=-1)
    northern = jnp.concatenate([centre[..., 1:], zero_col], axis=-1)
    result = centre - jnp.maximum(flow_lon, 0.0) * (centre - western)
    result = result - jnp.minimum(flow_lon, 0.0) * (eastern - centre)
    result = result - jnp.maximum(flow_lat, 0.0) * (centre - south_boundary)
    result = result - jnp.minimum(flow_lat, 0.0) * (northern - centre)
    return result


def per_device(
    members,
    courant_lon,
    courant_lat,
    vert_modes,
    horiz_modes,
    obs_index,
    obs_count,
    obs_value,
    obs_var,
):
    mem_dev, layer_tally, band_width, lat_rows = members.shape
    sample_tally_overall = mem_dev * lax.axis_size("mem")
    rim_depth = ADV_STEPS
    stacked = jnp.concatenate(
        [members.reshape(mem_dev * layer_tally, band_width, lat_rows), courant_lon, courant_lat],
        axis=0,
    )
    extended = padded(stacked, (("lon", 1),), rim_depth)
    split_at = mem_dev * layer_tally
    prognostic_vector = extended[:split_at].reshape(
        mem_dev, layer_tally, band_width + 2 * rim_depth, lat_rows
    )
    flow_lon_ext = extended[split_at : split_at + layer_tally]
    meridional_wind_padded = extended[split_at + layer_tally :]
    for section in range(rim_depth):
        out_cols = band_width + 2 * (rim_depth - 1 - section)
        first_col = section + 1
        prognostic_vector = update(
            prognostic_vector[:, :, 1 : out_cols + 1],
            prognostic_vector[:, :, 0:out_cols],
            prognostic_vector[:, :, 2 : out_cols + 2],
            flow_lon_ext[:, first_col : first_col + out_cols],
            meridional_wind_padded[:, first_col : first_col + out_cols],
        )
    sample_centroid = lax.psum(jnp.sum(prognostic_vector, axis=0), "mem") / sample_tally_overall
    sample_departure = prognostic_vector - sample_centroid[None]
    norm_scale = (sample_tally_overall - 1) ** (-0.5)
    obs_slots = obs_index.shape[0]
    band_cells = band_width * lat_rows
    level_idx = obs_index // band_cells
    within = obs_index % band_cells
    anomaly_obs = jnp.take(sample_departure.reshape(mem_dev, -1), obs_index, axis=1)
    mean_obs = jnp.take(sample_centroid.reshape(-1), obs_index)
    vert_obs = jnp.take(vert_modes, level_idx, axis=1)
    horiz_obs = jnp.take(horiz_modes.reshape(KH, -1), within, axis=1)
    modes_obs = (vert_obs[:, None, :] * horiz_obs[None, :, :]).reshape(KV * KH, obs_slots)
    live_mask = (jnp.arange(obs_slots, dtype=jnp.int32) < obs_count[0]).astype(jnp.float32)
    obs_perts = (
        anomaly_obs[:, None, :] * modes_obs[None, :, :] * (live_mask * norm_scale)[None, None, :]
    )
    obs_perts = obs_perts.reshape(mem_dev * KV * KH, obs_slots)
    inv_var = live_mask / obs_var
    innovation = obs_value - mean_obs
    all_perts = lax.all_gather(obs_perts, "mem", axis=0, tiled=True)
    gram_part = jnp.dot(all_perts * inv_var[None, :], all_perts.T, precision=lax.Precision.HIGHEST)
    side_part = jnp.dot(all_perts, inv_var * innovation, precision=lax.Precision.HIGHEST)
    gram_matrix, right_side = lax.psum((gram_part, side_part), "lon")
    system = jnp.eye(gram_matrix.shape[0], dtype=jnp.float32) + gram_matrix
    factor = jnp.linalg.cholesky(system)
    weights = jax.scipy.linalg.cho_solve((factor, True), right_side)
    w_mat = weights.reshape(sample_tally_overall, KV * KH)
    w_local = lax.dynamic_slice_in_dim(w_mat, lax.axis_index("mem") * mem_dev, mem_dev, 0)
    mode_coef = jnp.einsum(
        "mk,mlij->klij", w_local, sample_departure, precision=lax.Precision.HIGHEST
    )
    mode_coef = mode_coef.reshape(KV, KH, layer_tally, band_width, lat_rows)
    inc_part = (
        jnp.einsum(
            "al,bij,ablij->lij", vert_modes, horiz_modes, mode_coef, precision=lax.Precision.HIGHEST
        )
        * norm_scale
    )
    posterior_adjustment = lax.psum(inc_part, "mem")
    return (prognostic_vector, sample_centroid + posterior_adjustment)


def choose(*args):
    mem_dev, layers, width, lats = args[0].shape
    n_lon = lax.axis_size("lon")
    n_mem = lax.axis_size("mem")
    fits = (
        mem_dev == 8
        and layers == 4
        and n_mem == layers
        and n_lon == 8
        and width % 8 == 0
        and lats == 256
        and args[5].shape[0] % (GROUPS * PIECE) == 0
    )
    return fast_device(*args) if fits else per_device(*args)


def solution(mesh):
    placed = (
        P("mem", None, "lon", None),
        P(None, "lon", None),
        P(None, "lon", None),
        P(),
        P(None, "lon", None),
        P("lon"),
        P("lon"),
        P("lon"),
        P("lon"),
    )
    return jax.shard_map(
        choose,
        mesh=mesh,
        in_specs=placed,
        out_specs=(P("mem", None, "lon", None), P(None, "lon", None)),
        check_vma=False,
    )
```

```python
import functools

import jax
import jax.numpy as jnp
from jax import lax
from jax.experimental import pallas as pl
from jax.experimental.pallas import tpu as pltpu
from jax.sharding import PartitionSpec as P

KV = 2
KH = 4
ADV_STEPS = 2
MODES = KV * KH
PAIRS = ((0, 0), (0, 1), (1, 1))
MESH = pl.DeviceIdType.MESH
VMEM_LIMIT = 24 * 1024 * 1024
HIGHEST = lax.Precision.HIGHEST
PIECE = 512
GROUPS = 4


def vmem():
    return pl.BlockSpec(memory_space=pltpu.VMEM)


def smem():
    return pl.BlockSpec(memory_space=pltpu.SMEM)


def hbm():
    return pl.BlockSpec(memory_space=pltpu.HBM)


def stay(x):
    return pltpu.with_memory_space_constraint(x, pltpu.HBM)


def greet(peers):
    barrier = pltpu.get_barrier_semaphore()
    for peer in peers:
        pl.semaphore_signal(barrier, inc=1, device_id=peer, device_id_type=MESH)
    return barrier


def axis_peers(axis, count):
    me = lax.axis_index(axis)
    return [{axis: lax.rem(me + d, count)} for d in range(1, count)]


def send(src, dst, send_sem, recv_sem, peer):
    copy = pltpu.make_async_remote_copy(
        src_ref=src, dst_ref=dst, send_sem=send_sem, recv_sem=recv_sem,
        device_id=peer, device_id_type=MESH,
    )
    copy.start()
    return copy


def bring(src, dst, sem):
    copy = pltpu.make_async_copy(src, dst, sem)
    copy.start()
    return copy


def two_terms(x):
    high = x.astype(jnp.bfloat16)
    return high, (x - high.astype(jnp.float32)).astype(jnp.bfloat16)


def front_kernel(
    n_lon, n_mem, norm,
    members, cx, cy, horiz, index, value_in, var_in, vert_in, count,
    prior, analysis,
    level, system, work, ext, cx_ext, cy_ext, belt, sides, cx_rim, cy_rim, modes, cells, value, var, vert, edge_out, edge_in, spots, terms, gathered,
    obs_horiz, total, staged, heard,
    in_sem, edge_send, edge_recv, obs_send, obs_recv, far_sem,
    part_send, part_recv, all_send, all_recv, level_send, level_recv, field_send, field_recv,
):
    mem_dev, layers, width, lats = members.shape
    stack = mem_dev * layers
    slots = index.shape[1]
    tiles = width // 8
    shift = lats.bit_length() - 1
    me = lax.axis_index("lon")
    me_mem = lax.axis_index("mem")
    left = {"lon": lax.rem(me + n_lon - 1, n_lon)}
    right = {"lon": lax.rem(me + 1, n_lon)}
    others = axis_peers("mem", n_mem)

    states = [
        bring(members.at[m], ext.at[pl.ds(m * layers, layers)], in_sem.at[m])
        for m in range(mem_dev)
    ]
    flows = [
        bring(cx, cx_ext, in_sem.at[mem_dev]),
        bring(cy, cy_ext, in_sem.at[mem_dev + 1]),
    ]
    places = bring(index, cells, in_sem.at[mem_dev + 2])
    shapes = bring(horiz, modes, in_sem.at[mem_dev + 3])
    observed = [
        bring(src, dst, in_sem.at[mem_dev + 4 + i])
        for i, (src, dst) in enumerate(((value_in, value), (var_in, var), (vert_in, vert)))
    ]
    barrier = greet([left, right] + others)
    for copy in states + flows:
        copy.wait()
    for side, (first, second, rim) in enumerate(((0, 1, 0), (width - 2, width - 1, width - 1))):
        edge_out[side, 0:stack, :] = ext[:, first, :]
        edge_out[side, stack : 2 * stack, :] = ext[:, second, :]
        edge_out[side, 2 * stack : 2 * stack + layers, :] = cx_ext[:, rim, :]
        edge_out[side, 2 * stack + layers : 2 * stack + 2 * layers, :] = cy_ext[:, rim, :]
    pl.semaphore_wait(barrier, 2 + len(others))
    to_left = send(edge_out.at[0], edge_in.at[1], edge_send.at[0], edge_recv.at[1], left)
    to_right = send(edge_out.at[1], edge_in.at[0], edge_send.at[1], edge_recv.at[0], right)

    places.wait()
    shapes.wait()
    sub = lax.broadcasted_iota(jnp.int32, (8, 128), 0)
    lat_row = lax.broadcasted_iota(jnp.int32, (lats, PIECE), 0)

    def rows_of(start):
        return jnp.broadcast_to(lax.shift_right_logical(cells[:, pl.ds(start, 128)], shift), (8, 128))

    def picked(found, tile, wanted, blocks, origin):
        total = [jnp.zeros((8, 128), jnp.float32)] * blocks
        for t, rows in wanted:
            here = tile == t
            total = [
                jnp.where(here, found[rows + origin(k) : rows + origin(k) + 8], x)
                for k, x in enumerate(total)
            ]
        return total

    def settle(values, sublane):
        here = sub == sublane
        sums = [jnp.sum(jnp.where(here, x, 0.0), axis=0, keepdims=True) for x in values]
        while len(sums) < 8:
            sums.append(jnp.zeros((1, 128), jnp.float32))
        return jnp.concatenate(sums, axis=0)

    mode_terms = jnp.concatenate(two_terms(modes[...].reshape(KH * width, lats)), axis=1)

    def spot(c, carry):
        start = pl.multiple_of(c * PIECE, PIECE)
        lat = jnp.bitwise_and(cells[:, pl.ds(start, PIECE)], lats - 1)
        mask = jnp.where(lat_row == lat, 1.0, 0.0).astype(jnp.bfloat16)
        spots[0:lats, pl.ds(start, PIECE)] = mask
        spots[lats : 2 * lats, pl.ds(start, PIECE)] = mask
        found = jnp.dot(
            mode_terms, jnp.concatenate([mask, mask], axis=0), preferred_element_type=jnp.float32
        )
        for h in range(PIECE // 128):
            low = pl.multiple_of(start + h * 128, 128)
            row = rows_of(low)
            for l in range(1, layers):
                row = jnp.where(rows_of(low) >= l * width, rows_of(low) - l * width, row)
            tile = lax.shift_right_logical(row, 3)
            part = found[:, h * 128 : (h + 1) * 128]
            values = picked(part, tile, [(t, t * 8) for t in range(tiles)], KH, lambda k: k * width)
            obs_horiz[:, pl.ds(low, 128)] = settle(values, jnp.bitwise_and(row, 7))
        return carry

    lax.fori_loop(0, slots // PIECE, spot, 0)

    lane = lax.broadcasted_iota(jnp.int32, (8, lats), 1)
    height = lax.broadcasted_iota(jnp.int32, (8, lats), 0)

    def advance(q, west, east, flows):
        done = []
        for t, x in enumerate(q):
            south = jnp.where(lane == 0, 0.0, pltpu.roll(x, 1, 1))
            north = jnp.where(lane == lats - 1, 0.0, pltpu.roll(x, lats - 1, 1))
            r = x - flows[0][t] * (x - west[t])
            r = r - flows[1][t] * (east[t] - x)
            r = r - flows[2][t] * (x - south)
            done.append(r - flows[3][t] * (north - x))
        return done

    def flows_of(cx_ref, cy_ref, l, count):
        x = [cx_ref[l, t * 8 : t * 8 + 8, :] for t in range(count)]
        y = [cy_ref[l, t * 8 : t * 8 + 8, :] for t in range(count)]
        return [
            [jnp.maximum(v, 0.0) for v in x], [jnp.minimum(v, 0.0) for v in x],
            [jnp.maximum(v, 0.0) for v in y], [jnp.minimum(v, 0.0) for v in y],
        ]

    def ends(q):
        return jnp.where(height < 2, pltpu.roll(q[-1], 2, 0), pltpu.roll(q[0], 6, 0))

    def beyond(q):
        return jnp.where(height == 0, pltpu.roll(q[-1], 3, 0), pltpu.roll(q[0], 5, 0))

    for l in range(layers):
        flows = flows_of(cx_ext, cy_ext, l, tiles)
        for source, target in ((cx_ext, cx_rim), (cy_ext, cy_rim)):
            target[l] = ends([source[l, 0:8, :], source[l, width - 8 : width, :]])

        def step(m, carry, l=l, flows=flows):
            f = m * layers + l
            q = [ext[f, t * 8 : t * 8 + 8, :] for t in range(tiles)]
            belt[f] = ends(q)
            for k in range(ADV_STEPS):
                sides[k, f] = beyond(q)
                low = [pltpu.roll(x, 1, 0) for x in q]
                high = [pltpu.roll(x, 7, 0) for x in q]
                west = [jnp.where(height == 0, low[t - 1], x) for t, x in enumerate(low)]
                east = [jnp.where(height == 7, high[(t + 1) % tiles], x) for t, x in enumerate(high)]
                q = advance(q, west, east, flows)
            prior[l, m] = jnp.concatenate(q, axis=0)
            return carry

        lax.fori_loop(0, mem_dev, step, 0, unroll=4)

    to_left.wait_recv()
    to_right.wait_recv()
    for d in (2, n_lon - 2):
        pl.semaphore_signal(
            far_sem, inc=1, device_id={"lon": lax.rem(me + d, n_lon)}, device_id_type=MESH
        )
    for place, side, at in ((2, 1, 0), (3, 1, stack), (4, 0, 0), (5, 0, stack)):
        belt[:, place, :] = edge_in[side, at : at + stack, :]
    for place, side in ((2, 1), (5, 0)):
        cx_rim[:, place, :] = edge_in[side, 2 * stack : 2 * stack + layers, :]
        cy_rim[:, place, :] = edge_in[side, 2 * stack + layers : 2 * stack + 2 * layers, :]

    for l in range(layers):
        flows = flows_of(cx_rim, cy_rim, l, 1)

        def finish(pair, carry, l=l, flows=flows):
            inner = []
            for j in range(2):
                m = pair * 2 + j
                f = m * layers + l
                q = belt[f]
                for k in range(ADV_STEPS):
                    side = sides[k, f]
                    west = jnp.where(height == 0, side, pltpu.roll(q, 1, 0))
                    east = jnp.where(height == 7, side, pltpu.roll(q, 7, 0))
                    q = advance([q], [west], [east], flows)[0]
                first = jnp.where(height < 2, pltpu.roll(q, 2, 0), prior[l, m, 0:8, :])
                final = jnp.where(height >= 6, pltpu.roll(q, 6, 0), prior[l, m, width - 8 : width, :])
                prior[l, m, 0:8, :] = first
                prior[l, m, width - 8 : width, :] = final
                inner += [first, prior[l, m, 8 : width - 8, :], final]
            start = pl.multiple_of((l * mem_dev + pair * 2) * width, 16)
            high, low = two_terms(jnp.concatenate(inner, axis=0))
            terms[pl.ds(start, 2 * width), 0:lats] = high
            terms[pl.ds(start, 2 * width), lats : 2 * lats] = low
            return carry

        lax.fori_loop(0, mem_dev // 2, finish, 0, unroll=4)

    wanted = [(l * tiles + t, l * mem_dev * width + t * 8) for l in range(layers) for t in range(tiles)]

    def gather(c, carry):
        start = pl.multiple_of(c * PIECE, PIECE)
        found = jnp.dot(
            terms[...], spots[:, pl.ds(start, PIECE)], preferred_element_type=jnp.float32
        )
        for h in range(PIECE // 128):
            low = pl.multiple_of(start + h * 128, 128)
            row = rows_of(low)
            part = found[:, h * 128 : (h + 1) * 128]
            tile = lax.shift_right_logical(row, 3)
            values = picked(part, tile, wanted, mem_dev, lambda k: k * width)
            gathered[me_mem, :, pl.ds(low, 128)] = settle(values, jnp.bitwise_and(row, 7))
        return carry

    span = slots // GROUPS
    steps = span // PIECE
    copies = []
    for c in range(GROUPS):
        lax.fori_loop(c * steps, (c + 1) * steps, gather, 0)
        piece = gathered.at[me_mem, :, pl.ds(c * span, span)]
        for d, peer in enumerate(others):
            copies.append(send(piece, piece, obs_send.at[c, d], obs_recv.at[c, d], peer))
    early = 4
    shares = [
        send(
            prior.at[peer["mem"], pl.ds(0, early)], level.at[me_mem, pl.ds(0, early)],
            level_send.at[0, d], level_recv.at[0, d], peer,
        )
        for d, peer in enumerate(others)
    ]
    level[me_mem] = prior[me_mem]

    members_all = n_mem * mem_dev
    for copy in observed:
        copy.wait()
    slot = lax.broadcasted_iota(jnp.int32, (1, span), 1)
    head = lax.broadcasted_iota(jnp.int32, (8, span), 0)
    factors = [[jnp.broadcast_to(vert[a : a + 1, l : l + 1], (1, span)) for l in range(layers)] for a in range(KV)]
    contract = (((1,), (1,)), ((), ()))

    def part(c):
        at = pl.ds(c * span, span)
        states = gathered[:, :, at].reshape(members_all, span)
        centre = jnp.sum(states, axis=0, keepdims=True) / members_all
        anomaly = states - centre
        mine = gathered[me_mem, :, at] - centre
        cell = cells[:, at]
        v = []
        for a in range(KV):
            x = factors[a][0]
            for l in range(1, layers):
                x = jnp.where(cell >= l * width * lats, factors[a][l], x)
            v.append(x)
        inv_var = jnp.where(slot + c * span < count[0], 1.0, 0.0) / var[:, at]
        drive = inv_var * (value[:, at] - centre) * norm
        weight = inv_var * (norm * norm)
        local_modes = obs_horiz[0:KH, at]
        wide = jnp.concatenate([anomaly * local_modes[b : b + 1] for b in range(KH)], axis=0)
        own = jnp.concatenate([mine * local_modes[b : b + 1] for b in range(KH)], axis=0)
        drives = jnp.where(head == 0, v[0] * drive, jnp.where(head == 1, v[1] * drive, 0.0))
        narrow = jnp.concatenate(
            [own * (v[a] * v[e] * weight) for a, e in PAIRS] + [drives, jnp.zeros_like(drives)], axis=0
        )
        wide_high, wide_low = two_terms(wide)
        narrow_high, narrow_low = two_terms(narrow)
        first = lax.dot_general(
            jnp.concatenate([narrow_high, narrow_low], axis=0), wide_high, contract,
            preferred_element_type=jnp.float32,
        )
        second = lax.dot_general(
            narrow_high, wide_low, contract, preferred_element_type=jnp.float32
        )
        rows = narrow.shape[0]
        return first[0:rows] + first[rows : 2 * rows] + second

    peers = len(others)
    for c in range(GROUPS):
        for copy in copies[c * peers : (c + 1) * peers]:
            copy.wait_recv()
        if c == 0:
            total[...] = part(c)
        else:
            total[...] += part(c)
    local = KH * mem_dev
    lane = lax.broadcasted_iota(jnp.int32, (8, 128), 1)

    def block(pair, b):
        return total[pair * local + b * 8 : pair * local + b * 8 + 8, :]

    for pair in range(3):
        staged[pair] = block(pair, 0)
        staged[3 + pair] = jnp.where(lane < 32, pltpu.roll(block(pair, 3), 32, 1), block(pair, 1))
    staged[6] = jnp.where(lane < 64, pltpu.roll(block(1, 2), 64, 1), block(0, 2))
    side = total[3 * local : 3 * local + 8, :]
    other = pltpu.roll(pltpu.roll(side, 64, 1), KV, 0)
    staged[7] = jnp.where(lane < 64, jnp.where(sub < KV, side, other), block(2, 2))

    pl.semaphore_wait(far_sem, 2)
    parts = [
        send(staged.at[peer["lon"]], heard.at[me], part_send.at[d], part_recv.at[d], peer)
        for d, peer in enumerate(axis_peers("lon", n_lon))
    ]
    heard[me] = staged[me]
    for copy in parts:
        copy.wait_recv()
    summed = heard[0]
    for d in range(1, n_lon):
        summed = summed + heard[d]
    core, row = lax.rem(me, 2), lax.div(me, 2)
    system[core, me_mem, row] = summed
    piece = system.at[core, me_mem, row]
    spread = []
    for hop in range(1, n_lon // 2 * n_mem):
        peer = {
            "lon": lax.rem(me + hop // n_mem * 2, n_lon),
            "mem": lax.rem(me_mem + hop % n_mem, n_mem),
        }
        spread.append(send(piece, piece, all_send.at[hop], all_recv.at[hop], peer))
    for copy in spread:
        copy.wait_recv()
    half = system.at[core]
    spread.append(send(half, half, all_send.at[0], all_recv.at[0], {"lon": me + 1 - 2 * core}))
    spread[-1].wait_recv()

    shares += [
        send(
            prior.at[peer["mem"], pl.ds(early, mem_dev - early)], level.at[me_mem, pl.ds(early, mem_dev - early)],
            level_send.at[1, d], level_recv.at[1, d], peer,
        )
        for d, peer in enumerate(others)
    ]
    size = members_all * MODES
    columns = size + 128
    unpack(system, work, size)
    eliminate(work, size, columns)
    half = size // KV
    lines = []
    for a in range(KV):
        x = jnp.broadcast_to(vert[a : a + 1, 0:1], (1, 128))
        for l in range(1, layers):
            x = jnp.where(me_mem == l, jnp.broadcast_to(vert[a : a + 1, l : l + 1], (1, 128)), x)
        lines.append(x)
    mixed = lines[0] * work[0:half, size:columns] + lines[1] * work[half:size, size:columns]
    for copy in shares:
        copy.wait_recv()
    centre = level[0, 0]
    for m in range(1, members_all):
        centre = centre + level[m // mem_dev, m % mem_dev]
    centre = centre / members_all
    increment = jnp.zeros_like(centre)
    for m in range(members_all):
        coef = None
        for b in range(KH):
            w = mixed[b * members_all + m : b * members_all + m + 1, :]
            w = jnp.concatenate([w] * (lats // 128), axis=1)
            coef = w * modes[b] if coef is None else coef + w * modes[b]
        increment = increment + coef * (level[m // mem_dev, m % mem_dev] - centre)
    analysis[me_mem] = centre + increment * norm
    piece = analysis.at[me_mem]
    fields = [
        send(piece, piece, field_send.at[d], field_recv.at[d], peer)
        for d, peer in enumerate(others)
    ]
    for copy in fields:
        copy.wait_recv()
    to_left.wait_send()
    to_right.wait_send()
    for copy in copies + shares + parts + spread + fields:
        copy.wait_send()


def unpack(system, work, size):
    lane = lax.broadcasted_iota(jnp.int32, (32, 128), 1)
    unit = jnp.where(
        lax.broadcasted_iota(jnp.int32, (128, 128), 0) == lax.broadcasted_iota(jnp.int32, (128, 128), 1),
        1.0, 0.0,
    )
    groups = system.shape[1]

    def take(t):
        return jnp.concatenate([system[t % 2, g, t // 2] for g in range(groups)], axis=0)

    last = [pltpu.roll(take(6), 64, 1), take(7)]
    thirds = [take(6), last[0], last[1]]
    for pair, (a, e) in enumerate(PAIRS):
        first, second, third = take(pair), take(3 + pair), thirds[pair]
        first_32, first_64, first_96 = (pltpu.roll(first, s, 1) for s in (96, 64, 32))
        second_32, second_64 = (pltpu.roll(second, s, 1) for s in (96, 64))
        third_32 = pltpu.roll(third, 96, 1)
        whole = jnp.concatenate(
            [
                first,
                jnp.where(lane < 32, first_32, second),
                jnp.where(lane < 32, first_64, jnp.where(lane < 64, second_32, third)),
                jnp.where(
                    lane < 32, first_96,
                    jnp.where(lane < 64, second_64, jnp.where(lane < 96, third_32, second_32)),
                ),
            ],
            axis=0,
        )
        if a == e:
            work[a * 128 : (a + 1) * 128, a * 128 : (a + 1) * 128] = whole + unit
        else:
            work[a * 128 : (a + 1) * 128, e * 128 : (e + 1) * 128] = whole
            work[e * 128 : (e + 1) * 128, a * 128 : (a + 1) * 128] = whole
    side = system[1, 0, 3]
    turned = pltpu.roll(side, 64, 1)
    narrow = lax.broadcasted_iota(jnp.int32, (1, 128), 1)
    for a in range(KV):
        line = jnp.where(narrow < 64, side[a : a + 1], turned[KV + a : KV + a + 1])
        work[a * 128 : (a + 1) * 128, size : size + 128] = jnp.broadcast_to(line, (128, 128)).T


def row_of(x, j):
    return jnp.broadcast_to(x[j : j + 1, :], (8, 128))


def lanes_of(x, start):
    return [jnp.broadcast_to(x[:, start + c : start + c + 1], (8, 128)) for c in range(8)]


def added(terms):
    while len(terms) > 1:
        terms = [x + y for x, y in zip(terms[::2], terms[1::2])] + terms[len(terms) // 2 * 2 :]
    return terms[0]


def three_terms(x):
    high = x.astype(jnp.bfloat16)
    rest = x - high.astype(jnp.float32)
    middle = rest.astype(jnp.bfloat16)
    return high, middle, (rest - middle.astype(jnp.float32)).astype(jnp.bfloat16)


def wide_product(x, y):
    copies = x.shape[1] // y.shape[0]
    x0, x1, x2 = three_terms(x)
    y0, y1, y2 = three_terms(y)
    stack = [t for t in (y0, y0, y1, y1, y2, y0) for _ in range(copies)]
    return jnp.dot(
        jnp.concatenate([x0, x1, x0, x1, x0, x2], axis=1), jnp.concatenate(stack, axis=0),
        preferred_element_type=jnp.float32,
    )


def packed_product(x, y, shift):
    depth = y.shape[0]
    parts = 128 // depth
    part = lax.broadcasted_iota(jnp.int32, x.shape, 1) // depth
    own = x
    for k in range(1, parts):
        x = jnp.where(part == (shift // depth + k) % parts, pltpu.roll(own, k * depth, 1), x)
    x0, x1, x2 = (t.astype(jnp.float32) for t in three_terms(x))
    y0, y1, y2 = three_terms(y)
    pairs = [(x0, y0), (x1, y0), (x0, y1), (x1, y1), (x0, y2), (x2, y0)]
    pairs += [(jnp.zeros_like(x0), y0)] * (-len(pairs) % parts)
    left, right = [], []
    for at in range(0, len(pairs), parts):
        tile = pairs[at][0]
        for k in range(1, parts):
            tile = jnp.where(part == k, pairs[at + k][0], tile)
        left.append(tile.astype(jnp.bfloat16))
        right += [t for _, t in pairs[at : at + parts]]
    return jnp.dot(
        jnp.concatenate(left, axis=1), jnp.concatenate(right, axis=0),
        preferred_element_type=jnp.float32,
    )


def eliminate(work, size, columns):
    depth = 64
    blocks = depth // 8
    sub = lax.broadcasted_iota(jnp.int32, (8, 128), 0)
    lanes = lax.broadcasted_iota(jnp.int32, (8, 128), 1)
    for top in range(0, size, depth):
        low = top // 128 * 128
        shift = top - low
        mirror = (shift + 64) % 128
        inside = (lanes >= shift) & (lanes < shift + depth)
        panel = [
            jnp.where(
                inside, work[top + i * 8 : top + i * 8 + 8, low : low + 128],
                jnp.where(lanes - mirror == sub + i * 8, 1.0, 0.0),
            )
            for i in range(blocks)
        ]
        lead = lanes_of(panel[0], shift)
        for s in range(blocks):
            lane = shift + s * 8
            row = panel[s]
            ahead, corner, slope = [], [], []
            if s + 1 < blocks:
                ahead = lanes_of(row, lane + 8)
                corner = lanes_of(panel[s + 1], lane + 8)
                slope = lanes_of(panel[s + 1], lane)
            near = list(slope)
            scale = None
            for j in range(8):
                inv = 1.0 / row_of(lead[j], j)
                g = jnp.where(sub == j, 0.0, lead[j] * inv)
                h = slope[j] * inv if slope else None
                for c in range(j + 1, 8):
                    r = row_of(lead[c], j)
                    lead[c] = lead[c] - g * r
                    if slope:
                        slope[c] = slope[c] - h * r
                for c in range(len(ahead)):
                    r = row_of(ahead[c], j)
                    ahead[c] = ahead[c] - g * r
                    corner[c] = corner[c] - h * r
                row = row - g * row_of(row, j)
                scale = inv if scale is None else jnp.where(sub == j, inv, scale)
            lead = corner
            row = row * scale
            panel[s] = row
            spread = [row_of(row, j) for j in range(8)]
            for d in range(1, blocks):
                i = (s + d) % blocks
                factor = near if d == 1 and near else lanes_of(panel[i], lane)
                panel[i] = panel[i] - added([factor[j] * spread[j] for j in range(8)])
        image = (lanes >= mirror) & (lanes < mirror + depth)
        inverse = jnp.concatenate([jnp.where(image, x, 0.0) for x in panel], axis=0)
        first = (top + depth) // 128 * 128
        own = wide_product(inverse, work[top : top + depth, first:columns])
        others = [x for x in ((0, top), (top + depth, size)) if x[0] < x[1]]
        factor = jnp.concatenate([work[x:y, low : low + 128] for x, y in others], axis=0)
        change = packed_product(factor, own, shift)
        work[top : top + depth, first:columns] = own
        at = 0
        for x, y in others:
            work[x:y, first:columns] -= change[at : at + y - x]
            at += y - x


def store_kernel(prior, analysis, prior_out, analysis_out, sems):
    layers = prior.shape[0]
    copies = [bring(prior.at[l], prior_out.at[:, l], sems.at[l]) for l in range(layers)]
    copies.append(bring(analysis, analysis_out, sems.at[layers]))
    for copy in copies:
        copy.wait()


def params(collective=None):
    if collective is None:
        return pltpu.CompilerParams(vmem_limit_bytes=VMEM_LIMIT)
    return pltpu.CompilerParams(
        vmem_limit_bytes=VMEM_LIMIT, collective_id=collective, has_side_effects=True
    )


def fast_device(
    members, courant_lon, courant_lat, vert_modes, horiz_modes,
    obs_index, obs_count, obs_value, obs_var,
):
    f32 = jnp.float32
    bf16 = jnp.bfloat16
    mem_dev, layers, width, lats = members.shape
    n_lon = lax.axis_size("lon")
    n_mem = lax.axis_size("mem")
    total = mem_dev * n_mem
    size = total * MODES
    norm = (total - 1) ** (-0.5)
    slots = obs_index.shape[0]
    stack = mem_dev * layers
    index = obs_index.reshape(1, slots)
    dma = pltpu.SemaphoreType.DMA
    edge_rows = 2 * stack + 2 * layers
    prior, analysis = pl.pallas_call(
        functools.partial(front_kernel, n_lon, n_mem, norm),
        out_shape=(
            jax.ShapeDtypeStruct((layers, mem_dev, width, lats), f32),
            jax.ShapeDtypeStruct((layers, width, lats), f32),
        ),
        in_specs=[hbm()] * 8 + [smem()],
        out_specs=(vmem(),) * 2,
        scratch_shapes=[
            pltpu.VMEM((n_mem, mem_dev, width, lats), f32),
            pltpu.VMEM((2, n_mem, n_lon // 2, 8, 128), f32),
            pltpu.VMEM((size, size + 128), f32),
            pltpu.VMEM((stack, width, lats), f32),
            pltpu.VMEM((layers, width, lats), f32),
            pltpu.VMEM((layers, width, lats), f32),
            pltpu.VMEM((stack, 8, lats), f32),
            pltpu.VMEM((ADV_STEPS, stack, 8, lats), f32),
            pltpu.VMEM((layers, 8, lats), f32),
            pltpu.VMEM((layers, 8, lats), f32),
            pltpu.VMEM((KH, width, lats), f32),
            pltpu.VMEM((1, slots), jnp.int32),
            pltpu.VMEM((1, slots), f32),
            pltpu.VMEM((1, slots), f32),
            pltpu.VMEM((KV, layers), f32),
            pltpu.VMEM((2, edge_rows, lats), f32),
            pltpu.VMEM((2, edge_rows, lats), f32),
            pltpu.VMEM((2 * lats, slots), bf16),
            pltpu.VMEM((stack * width, 2 * lats), bf16),
            pltpu.VMEM((n_mem, mem_dev, slots), f32),
            pltpu.VMEM((8, slots), f32),
            pltpu.VMEM((3 * KH * mem_dev + 16, 128), f32),
            pltpu.VMEM((n_lon, 8, 128), f32),
            pltpu.VMEM((n_lon, 8, 128), f32),
            dma((mem_dev + 7,)),
            dma((2,)), dma((2,)),
            dma((GROUPS, n_mem - 1)), dma((GROUPS, n_mem - 1)),
            pltpu.SemaphoreType.REGULAR,
            dma((n_lon - 1,)), dma((n_lon - 1,)),
            dma((n_lon // 2 * n_mem,)), dma((n_lon // 2 * n_mem,)),
            dma((2, n_mem - 1)), dma((2, n_mem - 1)),
            dma((n_mem - 1,)), dma((n_mem - 1,)),
        ],
        compiler_params=params(1),
        name="front",
    )(
        *map(
            stay,
            (
                members, courant_lon, courant_lat, horiz_modes, index,
                obs_value.reshape(1, slots), obs_var.reshape(1, slots), vert_modes,
            ),
        ),
        obs_count,
    )
    return pl.pallas_call(
        store_kernel,
        out_shape=(
            jax.ShapeDtypeStruct((mem_dev, layers, width, lats), f32),
            jax.ShapeDtypeStruct((layers, width, lats), f32),
        ),
        in_specs=[vmem()] * 2,
        out_specs=(hbm(), hbm()),
        scratch_shapes=[dma((layers + 1,))],
        compiler_params=params(),
        name="store",
    )(prior, analysis)


def padded(block, sides, width):
    for axis, dim in sides:
        count = lax.axis_size(axis)
        forward = [(i, i + 1) for i in range(count - 1)]
        forward.append((count - 1, 0))
        backward = [(target, source) for source, target in forward]
        low = lax.ppermute(
            lax.slice_in_dim(block, block.shape[dim] - width, None, axis=dim), axis, forward
        )
        high = lax.ppermute(lax.slice_in_dim(block, 0, width, axis=dim), axis, backward)
        block = jnp.concatenate([low, block, high], axis=dim)
    return block


def update(centre, western, eastern, flow_lon, flow_lat):
    zero_col = jnp.zeros_like(centre[..., :1])
    south_boundary = jnp.concatenate([zero_col, centre[..., :-1]], axis=-1)
    northern = jnp.concatenate([centre[..., 1:], zero_col], axis=-1)
    result = centre - jnp.maximum(flow_lon, 0.0) * (centre - western)
    result = result - jnp.minimum(flow_lon, 0.0) * (eastern - centre)
    result = result - jnp.maximum(flow_lat, 0.0) * (centre - south_boundary)
    result = result - jnp.minimum(flow_lat, 0.0) * (northern - centre)
    return result


def per_device(
    members,
    courant_lon,
    courant_lat,
    vert_modes,
    horiz_modes,
    obs_index,
    obs_count,
    obs_value,
    obs_var,
):
    mem_dev, layer_tally, band_width, lat_rows = members.shape
    sample_tally_overall = mem_dev * lax.axis_size("mem")
    rim_depth = ADV_STEPS
    stacked = jnp.concatenate(
        [members.reshape(mem_dev * layer_tally, band_width, lat_rows), courant_lon, courant_lat],
        axis=0,
    )
    extended = padded(stacked, (("lon", 1),), rim_depth)
    split_at = mem_dev * layer_tally
    prognostic_vector = extended[:split_at].reshape(
        mem_dev, layer_tally, band_width + 2 * rim_depth, lat_rows
    )
    flow_lon_ext = extended[split_at : split_at + layer_tally]
    meridional_wind_padded = extended[split_at + layer_tally :]
    for section in range(rim_depth):
        out_cols = band_width + 2 * (rim_depth - 1 - section)
        first_col = section + 1
        prognostic_vector = update(
            prognostic_vector[:, :, 1 : out_cols + 1],
            prognostic_vector[:, :, 0:out_cols],
            prognostic_vector[:, :, 2 : out_cols + 2],
            flow_lon_ext[:, first_col : first_col + out_cols],
            meridional_wind_padded[:, first_col : first_col + out_cols],
        )
    sample_centroid = lax.psum(jnp.sum(prognostic_vector, axis=0), "mem") / sample_tally_overall
    sample_departure = prognostic_vector - sample_centroid[None]
    norm_scale = (sample_tally_overall - 1) ** (-0.5)
    obs_slots = obs_index.shape[0]
    band_cells = band_width * lat_rows
    level_idx = obs_index // band_cells
    within = obs_index % band_cells
    anomaly_obs = jnp.take(sample_departure.reshape(mem_dev, -1), obs_index, axis=1)
    mean_obs = jnp.take(sample_centroid.reshape(-1), obs_index)
    vert_obs = jnp.take(vert_modes, level_idx, axis=1)
    horiz_obs = jnp.take(horiz_modes.reshape(KH, -1), within, axis=1)
    modes_obs = (vert_obs[:, None, :] * horiz_obs[None, :, :]).reshape(KV * KH, obs_slots)
    live_mask = (jnp.arange(obs_slots, dtype=jnp.int32) < obs_count[0]).astype(jnp.float32)
    obs_perts = (
        anomaly_obs[:, None, :] * modes_obs[None, :, :] * (live_mask * norm_scale)[None, None, :]
    )
    obs_perts = obs_perts.reshape(mem_dev * KV * KH, obs_slots)
    inv_var = live_mask / obs_var
    innovation = obs_value - mean_obs
    all_perts = lax.all_gather(obs_perts, "mem", axis=0, tiled=True)
    gram_part = jnp.dot(all_perts * inv_var[None, :], all_perts.T, precision=lax.Precision.HIGHEST)
    side_part = jnp.dot(all_perts, inv_var * innovation, precision=lax.Precision.HIGHEST)
    gram_matrix, right_side = lax.psum((gram_part, side_part), "lon")
    system = jnp.eye(gram_matrix.shape[0], dtype=jnp.float32) + gram_matrix
    factor = jnp.linalg.cholesky(system)
    weights = jax.scipy.linalg.cho_solve((factor, True), right_side)
    w_mat = weights.reshape(sample_tally_overall, KV * KH)
    w_local = lax.dynamic_slice_in_dim(w_mat, lax.axis_index("mem") * mem_dev, mem_dev, 0)
    mode_coef = jnp.einsum(
        "mk,mlij->klij", w_local, sample_departure, precision=lax.Precision.HIGHEST
    )
    mode_coef = mode_coef.reshape(KV, KH, layer_tally, band_width, lat_rows)
    inc_part = (
        jnp.einsum(
            "al,bij,ablij->lij", vert_modes, horiz_modes, mode_coef, precision=lax.Precision.HIGHEST
        )
        * norm_scale
    )
    posterior_adjustment = lax.psum(inc_part, "mem")
    return (prognostic_vector, sample_centroid + posterior_adjustment)


def choose(*args):
    mem_dev, layers, width, lats = args[0].shape
    n_lon = lax.axis_size("lon")
    n_mem = lax.axis_size("mem")
    fits = (
        mem_dev == 8
        and layers == 4
        and n_mem == layers
        and n_lon == 8
        and width % 8 == 0
        and width > 16
        and lats == 256
        and args[5].shape[0] % (GROUPS * PIECE) == 0
    )
    return fast_device(*args) if fits else per_device(*args)


def solution(mesh):
    placed = (
        P("mem", None, "lon", None),
        P(None, "lon", None),
        P(None, "lon", None),
        P(),
        P(None, "lon", None),
        P("lon"),
        P("lon"),
        P("lon"),
        P("lon"),
    )
    return jax.shard_map(
        choose,
        mesh=mesh,
        in_specs=placed,
        out_specs=(P("mem", None, "lon", None), P(None, "lon", None)),
        check_vma=False,
    )
```

```python
import functools

import jax
import jax.numpy as jnp
from jax import lax
from jax.experimental import pallas as pl
from jax.experimental.pallas import tpu as pltpu
from jax.sharding import PartitionSpec as P

KV = 2
KH = 4
ADV_STEPS = 2
MODES = KV * KH
PAIRS = ((0, 0), (0, 1), (1, 1))
MESH = pl.DeviceIdType.MESH
VMEM_LIMIT = 24 * 1024 * 1024
HIGHEST = lax.Precision.HIGHEST
PIECE = 512
GROUPS = 4


def vmem():
    return pl.BlockSpec(memory_space=pltpu.VMEM)


def smem():
    return pl.BlockSpec(memory_space=pltpu.SMEM)


def hbm():
    return pl.BlockSpec(memory_space=pltpu.HBM)


def stay(x):
    return pltpu.with_memory_space_constraint(x, pltpu.HBM)


def greet(peers):
    barrier = pltpu.get_barrier_semaphore()
    for peer in peers:
        pl.semaphore_signal(barrier, inc=1, device_id=peer, device_id_type=MESH)
    return barrier


def axis_peers(axis, count):
    me = lax.axis_index(axis)
    return [{axis: lax.rem(me + d, count)} for d in range(1, count)]


def send(src, dst, send_sem, recv_sem, peer):
    copy = pltpu.make_async_remote_copy(
        src_ref=src, dst_ref=dst, send_sem=send_sem, recv_sem=recv_sem,
        device_id=peer, device_id_type=MESH,
    )
    copy.start()
    return copy


def bring(src, dst, sem):
    copy = pltpu.make_async_copy(src, dst, sem)
    copy.start()
    return copy


def two_terms(x):
    high = x.astype(jnp.bfloat16)
    return high, (x - high.astype(jnp.float32)).astype(jnp.bfloat16)


def front_kernel(
    n_lon, n_mem, norm,
    members, cx, cy, horiz, index, value_in, var_in, vert_in, count,
    prior, analysis,
    level, system, work, ext, cx_ext, cy_ext, belt, sides, cx_rim, cy_rim, modes, cells, value, var, vert, edge_out, edge_in, spots, terms, gathered,
    obs_horiz, total, staged, heard,
    in_sem, edge_send, edge_recv, obs_send, obs_recv, far_sem,
    part_send, part_recv, all_send, all_recv, level_send, level_recv, field_send, field_recv,
):
    mem_dev, layers, width, lats = members.shape
    stack = mem_dev * layers
    slots = index.shape[1]
    tiles = width // 8
    shift = lats.bit_length() - 1
    me = lax.axis_index("lon")
    me_mem = lax.axis_index("mem")
    left = {"lon": lax.rem(me + n_lon - 1, n_lon)}
    right = {"lon": lax.rem(me + 1, n_lon)}
    others = axis_peers("mem", n_mem)

    states = [
        bring(members.at[m], ext.at[pl.ds(m * layers, layers)], in_sem.at[m])
        for m in range(mem_dev)
    ]
    flows = [
        bring(cx, cx_ext, in_sem.at[mem_dev]),
        bring(cy, cy_ext, in_sem.at[mem_dev + 1]),
    ]
    places = bring(index, cells, in_sem.at[mem_dev + 2])
    shapes = bring(horiz, modes, in_sem.at[mem_dev + 3])
    observed = [
        bring(src, dst, in_sem.at[mem_dev + 4 + i])
        for i, (src, dst) in enumerate(((value_in, value), (var_in, var), (vert_in, vert)))
    ]
    barrier = greet([left, right] + others)
    for copy in states + flows:
        copy.wait()
    for side, (first, second, rim) in enumerate(((0, 1, 0), (width - 2, width - 1, width - 1))):
        edge_out[side, 0:stack, :] = ext[:, first, :]
        edge_out[side, stack : 2 * stack, :] = ext[:, second, :]
        edge_out[side, 2 * stack : 2 * stack + layers, :] = cx_ext[:, rim, :]
        edge_out[side, 2 * stack + layers : 2 * stack + 2 * layers, :] = cy_ext[:, rim, :]
    pl.semaphore_wait(barrier, 2 + len(others))
    to_left = send(edge_out.at[0], edge_in.at[1], edge_send.at[0], edge_recv.at[1], left)
    to_right = send(edge_out.at[1], edge_in.at[0], edge_send.at[1], edge_recv.at[0], right)

    places.wait()
    shapes.wait()
    sub = lax.broadcasted_iota(jnp.int32, (8, 128), 0)
    lat_row = lax.broadcasted_iota(jnp.int32, (lats, PIECE), 0)

    def rows_of(start):
        return jnp.broadcast_to(lax.shift_right_logical(cells[:, pl.ds(start, 128)], shift), (8, 128))

    def picked(found, tile, wanted, blocks, origin):
        total = [jnp.zeros((8, 128), jnp.float32)] * blocks
        for t, rows in wanted:
            here = tile == t
            total = [
                jnp.where(here, found[rows + origin(k) : rows + origin(k) + 8], x)
                for k, x in enumerate(total)
            ]
        return total

    def settle(values, sublane):
        here = sub == sublane
        sums = [jnp.sum(jnp.where(here, x, 0.0), axis=0, keepdims=True) for x in values]
        while len(sums) < 8:
            sums.append(jnp.zeros((1, 128), jnp.float32))
        return jnp.concatenate(sums, axis=0)

    mode_terms = jnp.concatenate(two_terms(modes[...].reshape(KH * width, lats)), axis=1)

    def spot(c, carry):
        start = pl.multiple_of(c * PIECE, PIECE)
        lat = jnp.bitwise_and(cells[:, pl.ds(start, PIECE)], lats - 1)
        mask = jnp.where(lat_row == lat, 1.0, 0.0).astype(jnp.bfloat16)
        spots[0:lats, pl.ds(start, PIECE)] = mask
        spots[lats : 2 * lats, pl.ds(start, PIECE)] = mask
        found = jnp.dot(
            mode_terms, jnp.concatenate([mask, mask], axis=0), preferred_element_type=jnp.float32
        )
        for h in range(PIECE // 128):
            low = pl.multiple_of(start + h * 128, 128)
            row = rows_of(low)
            for l in range(1, layers):
                row = jnp.where(rows_of(low) >= l * width, rows_of(low) - l * width, row)
            tile = lax.shift_right_logical(row, 3)
            part = found[:, h * 128 : (h + 1) * 128]
            values = picked(part, tile, [(t, t * 8) for t in range(tiles)], KH, lambda k: k * width)
            obs_horiz[:, pl.ds(low, 128)] = settle(values, jnp.bitwise_and(row, 7))
        return carry

    lax.fori_loop(0, slots // PIECE, spot, 0)

    lane = lax.broadcasted_iota(jnp.int32, (8, lats), 1)
    height = lax.broadcasted_iota(jnp.int32, (8, lats), 0)

    def advance(q, west, east, flows):
        done = []
        for t, x in enumerate(q):
            south = jnp.where(lane == 0, 0.0, pltpu.roll(x, 1, 1))
            north = jnp.where(lane == lats - 1, 0.0, pltpu.roll(x, lats - 1, 1))
            r = x - flows[0][t] * (x - west[t])
            r = r - flows[1][t] * (east[t] - x)
            r = r - flows[2][t] * (x - south)
            done.append(r - flows[3][t] * (north - x))
        return done

    def flows_of(cx_ref, cy_ref, l, count):
        x = [cx_ref[l, t * 8 : t * 8 + 8, :] for t in range(count)]
        y = [cy_ref[l, t * 8 : t * 8 + 8, :] for t in range(count)]
        return [
            [jnp.maximum(v, 0.0) for v in x], [jnp.minimum(v, 0.0) for v in x],
            [jnp.maximum(v, 0.0) for v in y], [jnp.minimum(v, 0.0) for v in y],
        ]

    def ends(q):
        return jnp.where(height < 2, pltpu.roll(q[-1], 2, 0), pltpu.roll(q[0], 6, 0))

    def beyond(q):
        return jnp.where(height == 0, pltpu.roll(q[-1], 3, 0), pltpu.roll(q[0], 5, 0))

    for l in range(layers):
        flows = flows_of(cx_ext, cy_ext, l, tiles)
        for source, target in ((cx_ext, cx_rim), (cy_ext, cy_rim)):
            target[l] = ends([source[l, 0:8, :], source[l, width - 8 : width, :]])

        def step(m, carry, l=l, flows=flows):
            f = m * layers + l
            q = [ext[f, t * 8 : t * 8 + 8, :] for t in range(tiles)]
            belt[f] = ends(q)
            for k in range(ADV_STEPS):
                sides[k, f] = beyond(q)
                low = [pltpu.roll(x, 1, 0) for x in q]
                high = [pltpu.roll(x, 7, 0) for x in q]
                west = [jnp.where(height == 0, low[t - 1], x) for t, x in enumerate(low)]
                east = [jnp.where(height == 7, high[(t + 1) % tiles], x) for t, x in enumerate(high)]
                q = advance(q, west, east, flows)
            prior[l, m] = jnp.concatenate(q, axis=0)
            return carry

        lax.fori_loop(0, mem_dev, step, 0, unroll=4)

    to_left.wait_recv()
    to_right.wait_recv()
    for d in (2, n_lon - 2):
        pl.semaphore_signal(
            far_sem, inc=1, device_id={"lon": lax.rem(me + d, n_lon)}, device_id_type=MESH
        )
    for place, side, at in ((2, 1, 0), (3, 1, stack), (4, 0, 0), (5, 0, stack)):
        belt[:, place, :] = edge_in[side, at : at + stack, :]
    for place, side in ((2, 1), (5, 0)):
        cx_rim[:, place, :] = edge_in[side, 2 * stack : 2 * stack + layers, :]
        cy_rim[:, place, :] = edge_in[side, 2 * stack + layers : 2 * stack + 2 * layers, :]

    for l in range(layers):
        flows = flows_of(cx_rim, cy_rim, l, 1)

        def finish(pair, carry, l=l, flows=flows):
            inner = []
            for j in range(2):
                m = pair * 2 + j
                f = m * layers + l
                q = belt[f]
                for k in range(ADV_STEPS):
                    side = sides[k, f]
                    west = jnp.where(height == 0, side, pltpu.roll(q, 1, 0))
                    east = jnp.where(height == 7, side, pltpu.roll(q, 7, 0))
                    q = advance([q], [west], [east], flows)[0]
                first = jnp.where(height < 2, pltpu.roll(q, 2, 0), prior[l, m, 0:8, :])
                final = jnp.where(height >= 6, pltpu.roll(q, 6, 0), prior[l, m, width - 8 : width, :])
                prior[l, m, 0:8, :] = first
                prior[l, m, width - 8 : width, :] = final
                inner += [first, prior[l, m, 8 : width - 8, :], final]
            start = pl.multiple_of((l * mem_dev + pair * 2) * width, 16)
            high, low = two_terms(jnp.concatenate(inner, axis=0))
            terms[pl.ds(start, 2 * width), 0:lats] = high
            terms[pl.ds(start, 2 * width), lats : 2 * lats] = low
            return carry

        lax.fori_loop(0, mem_dev // 2, finish, 0, unroll=4)

    wanted = [(l * tiles + t, l * mem_dev * width + t * 8) for l in range(layers) for t in range(tiles)]

    def gather(c, carry):
        start = pl.multiple_of(c * PIECE, PIECE)
        found = jnp.dot(
            terms[...], spots[:, pl.ds(start, PIECE)], preferred_element_type=jnp.float32
        )
        for h in range(PIECE // 128):
            low = pl.multiple_of(start + h * 128, 128)
            row = rows_of(low)
            part = found[:, h * 128 : (h + 1) * 128]
            tile = lax.shift_right_logical(row, 3)
            values = picked(part, tile, wanted, mem_dev, lambda k: k * width)
            gathered[me_mem, :, pl.ds(low, 128)] = settle(values, jnp.bitwise_and(row, 7))
        return carry

    span = slots // GROUPS
    steps = span // PIECE
    copies = []
    for c in range(GROUPS):
        lax.fori_loop(c * steps, (c + 1) * steps, gather, 0)
        piece = gathered.at[me_mem, :, pl.ds(c * span, span)]
        for d, peer in enumerate(others):
            copies.append(send(piece, piece, obs_send.at[c, d], obs_recv.at[c, d], peer))
    early = 4
    shares = [
        send(
            prior.at[peer["mem"], pl.ds(0, early)], level.at[me_mem, pl.ds(0, early)],
            level_send.at[0, d], level_recv.at[0, d], peer,
        )
        for d, peer in enumerate(others)
    ]
    level[me_mem] = prior[me_mem]

    members_all = n_mem * mem_dev
    for copy in observed:
        copy.wait()
    slot = lax.broadcasted_iota(jnp.int32, (1, span), 1)
    head = lax.broadcasted_iota(jnp.int32, (8, span), 0)
    factors = [[jnp.broadcast_to(vert[a : a + 1, l : l + 1], (1, span)) for l in range(layers)] for a in range(KV)]
    contract = (((1,), (1,)), ((), ()))

    def part(c):
        at = pl.ds(c * span, span)
        states = gathered[:, :, at].reshape(members_all, span)
        centre = jnp.sum(states, axis=0, keepdims=True) / members_all
        anomaly = states - centre
        mine = gathered[me_mem, :, at] - centre
        cell = cells[:, at]
        v = []
        for a in range(KV):
            x = factors[a][0]
            for l in range(1, layers):
                x = jnp.where(cell >= l * width * lats, factors[a][l], x)
            v.append(x)
        inv_var = jnp.where(slot + c * span < count[0], 1.0, 0.0) / var[:, at]
        drive = inv_var * (value[:, at] - centre) * norm
        weight = inv_var * (norm * norm)
        local_modes = obs_horiz[0:KH, at]
        wide = jnp.concatenate([anomaly * local_modes[b : b + 1] for b in range(KH)], axis=0)
        own = jnp.concatenate([mine * local_modes[b : b + 1] for b in range(KH)], axis=0)
        drives = jnp.where(head == 0, v[0] * drive, jnp.where(head == 1, v[1] * drive, 0.0))
        narrow = jnp.concatenate(
            [own * (v[a] * v[e] * weight) for a, e in PAIRS] + [drives, jnp.zeros_like(drives)], axis=0
        )
        wide_high, wide_low = two_terms(wide)
        narrow_high, narrow_low = two_terms(narrow)
        first = lax.dot_general(
            jnp.concatenate([narrow_high, narrow_low], axis=0), wide_high, contract,
            preferred_element_type=jnp.float32,
        )
        second = lax.dot_general(
            narrow_high, wide_low, contract, preferred_element_type=jnp.float32
        )
        rows = narrow.shape[0]
        return first[0:rows] + first[rows : 2 * rows] + second

    peers = len(others)
    for c in range(GROUPS):
        for copy in copies[c * peers : (c + 1) * peers]:
            copy.wait_recv()
        if c == 0:
            total[...] = part(c)
        else:
            total[...] += part(c)
    local = KH * mem_dev
    lane = lax.broadcasted_iota(jnp.int32, (8, 128), 1)

    def block(pair, b):
        return total[pair * local + b * 8 : pair * local + b * 8 + 8, :]

    for pair in range(3):
        staged[pair] = block(pair, 0)
        staged[3 + pair] = jnp.where(lane < 32, pltpu.roll(block(pair, 3), 32, 1), block(pair, 1))
    staged[6] = jnp.where(lane < 64, pltpu.roll(block(1, 2), 64, 1), block(0, 2))
    side = total[3 * local : 3 * local + 8, :]
    other = pltpu.roll(pltpu.roll(side, 64, 1), KV, 0)
    staged[7] = jnp.where(lane < 64, jnp.where(sub < KV, side, other), block(2, 2))

    pl.semaphore_wait(far_sem, 2)
    parts = [
        send(staged.at[peer["lon"]], heard.at[me], part_send.at[d], part_recv.at[d], peer)
        for d, peer in enumerate(axis_peers("lon", n_lon))
    ]
    heard[me] = staged[me]
    for copy in parts:
        copy.wait_recv()
    summed = heard[0]
    for d in range(1, n_lon):
        summed = summed + heard[d]
    core, row = lax.rem(me, 2), lax.div(me, 2)
    system[core, me_mem, row] = summed
    piece = system.at[core, me_mem, row]
    spread = []
    for hop in range(1, n_lon // 2 * n_mem):
        peer = {
            "lon": lax.rem(me + hop // n_mem * 2, n_lon),
            "mem": lax.rem(me_mem + hop % n_mem, n_mem),
        }
        spread.append(send(piece, piece, all_send.at[hop], all_recv.at[hop], peer))
    for copy in spread:
        copy.wait_recv()
    half = system.at[core]
    spread.append(send(half, half, all_send.at[0], all_recv.at[0], {"lon": me + 1 - 2 * core}))
    spread[-1].wait_recv()

    shares += [
        send(
            prior.at[peer["mem"], pl.ds(early, mem_dev - early)], level.at[me_mem, pl.ds(early, mem_dev - early)],
            level_send.at[1, d], level_recv.at[1, d], peer,
        )
        for d, peer in enumerate(others)
    ]
    size = members_all * MODES
    columns = size + 128
    unpack(system, work, size)
    eliminate(work, size, columns)
    half = size // KV
    lines = []
    for a in range(KV):
        x = jnp.broadcast_to(vert[a : a + 1, 0:1], (1, 128))
        for l in range(1, layers):
            x = jnp.where(me_mem == l, jnp.broadcast_to(vert[a : a + 1, l : l + 1], (1, 128)), x)
        lines.append(x)
    mixed = lines[0] * work[0:half, size:columns] + lines[1] * work[half:size, size:columns]
    for copy in shares:
        copy.wait_recv()
    fields = []
    for t in range(tiles):
        at = pl.ds(t * 8, 8)
        centre = level[0, 0, at, :]
        for m in range(1, members_all):
            centre = centre + level[m // mem_dev, m % mem_dev, at, :]
        centre = centre / members_all
        increment = jnp.zeros_like(centre)
        for m in range(members_all):
            coef = None
            for b in range(KH):
                w = mixed[b * members_all + m : b * members_all + m + 1, :]
                w = jnp.concatenate([w] * (lats // 128), axis=1)
                shape = modes[b, at, :]
                coef = w * shape if coef is None else coef + w * shape
            increment = increment + coef * (level[m // mem_dev, m % mem_dev, at, :] - centre)
        analysis[me_mem, at, :] = centre + increment * norm
        piece = analysis.at[me_mem, at]
        fields += [
            send(piece, piece, field_send.at[t, d], field_recv.at[t, d], peer)
            for d, peer in enumerate(others)
        ]
    for copy in fields:
        copy.wait_recv()
    to_left.wait_send()
    to_right.wait_send()
    for copy in copies + shares + parts + spread + fields:
        copy.wait_send()


def unpack(system, work, size):
    lane = lax.broadcasted_iota(jnp.int32, (32, 128), 1)
    unit = jnp.where(
        lax.broadcasted_iota(jnp.int32, (128, 128), 0) == lax.broadcasted_iota(jnp.int32, (128, 128), 1),
        1.0, 0.0,
    )
    groups = system.shape[1]

    def take(t):
        return jnp.concatenate([system[t % 2, g, t // 2] for g in range(groups)], axis=0)

    last = [pltpu.roll(take(6), 64, 1), take(7)]
    thirds = [take(6), last[0], last[1]]
    for pair, (a, e) in enumerate(PAIRS):
        first, second, third = take(pair), take(3 + pair), thirds[pair]
        first_32, first_64, first_96 = (pltpu.roll(first, s, 1) for s in (96, 64, 32))
        second_32, second_64 = (pltpu.roll(second, s, 1) for s in (96, 64))
        third_32 = pltpu.roll(third, 96, 1)
        whole = jnp.concatenate(
            [
                first,
                jnp.where(lane < 32, first_32, second),
                jnp.where(lane < 32, first_64, jnp.where(lane < 64, second_32, third)),
                jnp.where(
                    lane < 32, first_96,
                    jnp.where(lane < 64, second_64, jnp.where(lane < 96, third_32, second_32)),
                ),
            ],
            axis=0,
        )
        if a == e:
            work[a * 128 : (a + 1) * 128, a * 128 : (a + 1) * 128] = whole + unit
        else:
            work[a * 128 : (a + 1) * 128, e * 128 : (e + 1) * 128] = whole
            work[e * 128 : (e + 1) * 128, a * 128 : (a + 1) * 128] = whole
    side = system[1, 0, 3]
    turned = pltpu.roll(side, 64, 1)
    narrow = lax.broadcasted_iota(jnp.int32, (1, 128), 1)
    for a in range(KV):
        line = jnp.where(narrow < 64, side[a : a + 1], turned[KV + a : KV + a + 1])
        work[a * 128 : (a + 1) * 128, size : size + 128] = jnp.broadcast_to(line, (128, 128)).T


def row_of(x, j):
    return jnp.broadcast_to(x[j : j + 1, :], (8, 128))


def lanes_of(x, start):
    return [jnp.broadcast_to(x[:, start + c : start + c + 1], (8, 128)) for c in range(8)]


def added(terms):
    while len(terms) > 1:
        terms = [x + y for x, y in zip(terms[::2], terms[1::2])] + terms[len(terms) // 2 * 2 :]
    return terms[0]


def three_terms(x):
    high = x.astype(jnp.bfloat16)
    rest = x - high.astype(jnp.float32)
    middle = rest.astype(jnp.bfloat16)
    return high, middle, (rest - middle.astype(jnp.float32)).astype(jnp.bfloat16)


def wide_product(x, y):
    copies = x.shape[1] // y.shape[0]
    x0, x1, x2 = three_terms(x)
    y0, y1, y2 = three_terms(y)
    stack = [t for t in (y0, y0, y1, y1, y2, y0) for _ in range(copies)]
    return jnp.dot(
        jnp.concatenate([x0, x1, x0, x1, x0, x2], axis=1), jnp.concatenate(stack, axis=0),
        preferred_element_type=jnp.float32,
    )


def packed_product(x, y, shift):
    depth = y.shape[0]
    parts = 128 // depth
    part = lax.broadcasted_iota(jnp.int32, x.shape, 1) // depth
    own = x
    for k in range(1, parts):
        x = jnp.where(part == (shift // depth + k) % parts, pltpu.roll(own, k * depth, 1), x)
    x0, x1, x2 = (t.astype(jnp.float32) for t in three_terms(x))
    y0, y1, y2 = three_terms(y)
    pairs = [(x0, y0), (x1, y0), (x0, y1), (x1, y1), (x0, y2), (x2, y0)]
    pairs += [(jnp.zeros_like(x0), y0)] * (-len(pairs) % parts)
    left, right = [], []
    for at in range(0, len(pairs), parts):
        tile = pairs[at][0]
        for k in range(1, parts):
            tile = jnp.where(part == k, pairs[at + k][0], tile)
        left.append(tile.astype(jnp.bfloat16))
        right += [t for _, t in pairs[at : at + parts]]
    return jnp.dot(
        jnp.concatenate(left, axis=1), jnp.concatenate(right, axis=0),
        preferred_element_type=jnp.float32,
    )


def eliminate(work, size, columns):
    depth = 64
    blocks = depth // 8
    sub = lax.broadcasted_iota(jnp.int32, (8, 128), 0)
    lanes = lax.broadcasted_iota(jnp.int32, (8, 128), 1)
    for top in range(0, size, depth):
        low = top // 128 * 128
        shift = top - low
        mirror = (shift + 64) % 128
        inside = (lanes >= shift) & (lanes < shift + depth)
        panel = [
            jnp.where(
                inside, work[top + i * 8 : top + i * 8 + 8, low : low + 128],
                jnp.where(lanes - mirror == sub + i * 8, 1.0, 0.0),
            )
            for i in range(blocks)
        ]
        lead = lanes_of(panel[0], shift)
        for s in range(blocks):
            lane = shift + s * 8
            row = panel[s]
            ahead, corner, slope = [], [], []
            if s + 1 < blocks:
                ahead = lanes_of(row, lane + 8)
                corner = lanes_of(panel[s + 1], lane + 8)
                slope = lanes_of(panel[s + 1], lane)
            near = list(slope)
            scale = None
            for j in range(8):
                inv = 1.0 / row_of(lead[j], j)
                g = jnp.where(sub == j, 0.0, lead[j] * inv)
                h = slope[j] * inv if slope else None
                for c in range(j + 1, 8):
                    r = row_of(lead[c], j)
                    lead[c] = lead[c] - g * r
                    if slope:
                        slope[c] = slope[c] - h * r
                for c in range(len(ahead)):
                    r = row_of(ahead[c], j)
                    ahead[c] = ahead[c] - g * r
                    corner[c] = corner[c] - h * r
                row = row - g * row_of(row, j)
                scale = inv if scale is None else jnp.where(sub == j, inv, scale)
            lead = corner
            row = row * scale
            panel[s] = row
            spread = [row_of(row, j) for j in range(8)]
            for d in range(1, blocks):
                i = (s + d) % blocks
                factor = near if d == 1 and near else lanes_of(panel[i], lane)
                panel[i] = panel[i] - added([factor[j] * spread[j] for j in range(8)])
        image = (lanes >= mirror) & (lanes < mirror + depth)
        inverse = jnp.concatenate([jnp.where(image, x, 0.0) for x in panel], axis=0)
        first = (top + depth) // 128 * 128
        own = wide_product(inverse, work[top : top + depth, first:columns])
        work[top : top + depth, first:columns] = own
        after = top + depth
        groups = [[(after, after + depth)]] if after < size else []
        rest = [x for x in ((0, top), (after + depth, size)) if x[0] < x[1]]
        for group in groups + ([rest] if rest else []):
            factor = jnp.concatenate([work[x:y, low : low + 128] for x, y in group], axis=0)
            change = packed_product(factor, own, shift)
            at = 0
            for x, y in group:
                work[x:y, first:columns] -= change[at : at + y - x]
                at += y - x


def store_kernel(prior, analysis, prior_out, analysis_out, sems):
    layers = prior.shape[0]
    copies = [bring(prior.at[l], prior_out.at[:, l], sems.at[l]) for l in range(layers)]
    copies.append(bring(analysis, analysis_out, sems.at[layers]))
    for copy in copies:
        copy.wait()


def params(collective=None):
    if collective is None:
        return pltpu.CompilerParams(vmem_limit_bytes=VMEM_LIMIT)
    return pltpu.CompilerParams(
        vmem_limit_bytes=VMEM_LIMIT, collective_id=collective, has_side_effects=True
    )


def fast_device(
    members, courant_lon, courant_lat, vert_modes, horiz_modes,
    obs_index, obs_count, obs_value, obs_var,
):
    f32 = jnp.float32
    bf16 = jnp.bfloat16
    mem_dev, layers, width, lats = members.shape
    n_lon = lax.axis_size("lon")
    n_mem = lax.axis_size("mem")
    total = mem_dev * n_mem
    size = total * MODES
    norm = (total - 1) ** (-0.5)
    slots = obs_index.shape[0]
    stack = mem_dev * layers
    index = obs_index.reshape(1, slots)
    dma = pltpu.SemaphoreType.DMA
    edge_rows = 2 * stack + 2 * layers
    prior, analysis = pl.pallas_call(
        functools.partial(front_kernel, n_lon, n_mem, norm),
        out_shape=(
            jax.ShapeDtypeStruct((layers, mem_dev, width, lats), f32),
            jax.ShapeDtypeStruct((layers, width, lats), f32),
        ),
        in_specs=[hbm()] * 8 + [smem()],
        out_specs=(vmem(),) * 2,
        scratch_shapes=[
            pltpu.VMEM((n_mem, mem_dev, width, lats), f32),
            pltpu.VMEM((2, n_mem, n_lon // 2, 8, 128), f32),
            pltpu.VMEM((size, size + 128), f32),
            pltpu.VMEM((stack, width, lats), f32),
            pltpu.VMEM((layers, width, lats), f32),
            pltpu.VMEM((layers, width, lats), f32),
            pltpu.VMEM((stack, 8, lats), f32),
            pltpu.VMEM((ADV_STEPS, stack, 8, lats), f32),
            pltpu.VMEM((layers, 8, lats), f32),
            pltpu.VMEM((layers, 8, lats), f32),
            pltpu.VMEM((KH, width, lats), f32),
            pltpu.VMEM((1, slots), jnp.int32),
            pltpu.VMEM((1, slots), f32),
            pltpu.VMEM((1, slots), f32),
            pltpu.VMEM((KV, layers), f32),
            pltpu.VMEM((2, edge_rows, lats), f32),
            pltpu.VMEM((2, edge_rows, lats), f32),
            pltpu.VMEM((2 * lats, slots), bf16),
            pltpu.VMEM((stack * width, 2 * lats), bf16),
            pltpu.VMEM((n_mem, mem_dev, slots), f32),
            pltpu.VMEM((8, slots), f32),
            pltpu.VMEM((3 * KH * mem_dev + 16, 128), f32),
            pltpu.VMEM((n_lon, 8, 128), f32),
            pltpu.VMEM((n_lon, 8, 128), f32),
            dma((mem_dev + 7,)),
            dma((2,)), dma((2,)),
            dma((GROUPS, n_mem - 1)), dma((GROUPS, n_mem - 1)),
            pltpu.SemaphoreType.REGULAR,
            dma((n_lon - 1,)), dma((n_lon - 1,)),
            dma((n_lon // 2 * n_mem,)), dma((n_lon // 2 * n_mem,)),
            dma((2, n_mem - 1)), dma((2, n_mem - 1)),
            dma((width // 8, n_mem - 1)), dma((width // 8, n_mem - 1)),
        ],
        compiler_params=params(1),
        name="front",
    )(
        *map(
            stay,
            (
                members, courant_lon, courant_lat, horiz_modes, index,
                obs_value.reshape(1, slots), obs_var.reshape(1, slots), vert_modes,
            ),
        ),
        obs_count,
    )
    return pl.pallas_call(
        store_kernel,
        out_shape=(
            jax.ShapeDtypeStruct((mem_dev, layers, width, lats), f32),
            jax.ShapeDtypeStruct((layers, width, lats), f32),
        ),
        in_specs=[vmem()] * 2,
        out_specs=(hbm(), hbm()),
        scratch_shapes=[dma((layers + 1,))],
        compiler_params=params(),
        name="store",
    )(prior, analysis)


def padded(block, sides, width):
    for axis, dim in sides:
        count = lax.axis_size(axis)
        forward = [(i, i + 1) for i in range(count - 1)]
        forward.append((count - 1, 0))
        backward = [(target, source) for source, target in forward]
        low = lax.ppermute(
            lax.slice_in_dim(block, block.shape[dim] - width, None, axis=dim), axis, forward
        )
        high = lax.ppermute(lax.slice_in_dim(block, 0, width, axis=dim), axis, backward)
        block = jnp.concatenate([low, block, high], axis=dim)
    return block


def update(centre, western, eastern, flow_lon, flow_lat):
    zero_col = jnp.zeros_like(centre[..., :1])
    south_boundary = jnp.concatenate([zero_col, centre[..., :-1]], axis=-1)
    northern = jnp.concatenate([centre[..., 1:], zero_col], axis=-1)
    result = centre - jnp.maximum(flow_lon, 0.0) * (centre - western)
    result = result - jnp.minimum(flow_lon, 0.0) * (eastern - centre)
    result = result - jnp.maximum(flow_lat, 0.0) * (centre - south_boundary)
    result = result - jnp.minimum(flow_lat, 0.0) * (northern - centre)
    return result


def per_device(
    members,
    courant_lon,
    courant_lat,
    vert_modes,
    horiz_modes,
    obs_index,
    obs_count,
    obs_value,
    obs_var,
):
    mem_dev, layer_tally, band_width, lat_rows = members.shape
    sample_tally_overall = mem_dev * lax.axis_size("mem")
    rim_depth = ADV_STEPS
    stacked = jnp.concatenate(
        [members.reshape(mem_dev * layer_tally, band_width, lat_rows), courant_lon, courant_lat],
        axis=0,
    )
    extended = padded(stacked, (("lon", 1),), rim_depth)
    split_at = mem_dev * layer_tally
    prognostic_vector = extended[:split_at].reshape(
        mem_dev, layer_tally, band_width + 2 * rim_depth, lat_rows
    )
    flow_lon_ext = extended[split_at : split_at + layer_tally]
    meridional_wind_padded = extended[split_at + layer_tally :]
    for section in range(rim_depth):
        out_cols = band_width + 2 * (rim_depth - 1 - section)
        first_col = section + 1
        prognostic_vector = update(
            prognostic_vector[:, :, 1 : out_cols + 1],
            prognostic_vector[:, :, 0:out_cols],
            prognostic_vector[:, :, 2 : out_cols + 2],
            flow_lon_ext[:, first_col : first_col + out_cols],
            meridional_wind_padded[:, first_col : first_col + out_cols],
        )
    sample_centroid = lax.psum(jnp.sum(prognostic_vector, axis=0), "mem") / sample_tally_overall
    sample_departure = prognostic_vector - sample_centroid[None]
    norm_scale = (sample_tally_overall - 1) ** (-0.5)
    obs_slots = obs_index.shape[0]
    band_cells = band_width * lat_rows
    level_idx = obs_index // band_cells
    within = obs_index % band_cells
    anomaly_obs = jnp.take(sample_departure.reshape(mem_dev, -1), obs_index, axis=1)
    mean_obs = jnp.take(sample_centroid.reshape(-1), obs_index)
    vert_obs = jnp.take(vert_modes, level_idx, axis=1)
    horiz_obs = jnp.take(horiz_modes.reshape(KH, -1), within, axis=1)
    modes_obs = (vert_obs[:, None, :] * horiz_obs[None, :, :]).reshape(KV * KH, obs_slots)
    live_mask = (jnp.arange(obs_slots, dtype=jnp.int32) < obs_count[0]).astype(jnp.float32)
    obs_perts = (
        anomaly_obs[:, None, :] * modes_obs[None, :, :] * (live_mask * norm_scale)[None, None, :]
    )
    obs_perts = obs_perts.reshape(mem_dev * KV * KH, obs_slots)
    inv_var = live_mask / obs_var
    innovation = obs_value - mean_obs
    all_perts = lax.all_gather(obs_perts, "mem", axis=0, tiled=True)
    gram_part = jnp.dot(all_perts * inv_var[None, :], all_perts.T, precision=lax.Precision.HIGHEST)
    side_part = jnp.dot(all_perts, inv_var * innovation, precision=lax.Precision.HIGHEST)
    gram_matrix, right_side = lax.psum((gram_part, side_part), "lon")
    system = jnp.eye(gram_matrix.shape[0], dtype=jnp.float32) + gram_matrix
    factor = jnp.linalg.cholesky(system)
    weights = jax.scipy.linalg.cho_solve((factor, True), right_side)
    w_mat = weights.reshape(sample_tally_overall, KV * KH)
    w_local = lax.dynamic_slice_in_dim(w_mat, lax.axis_index("mem") * mem_dev, mem_dev, 0)
    mode_coef = jnp.einsum(
        "mk,mlij->klij", w_local, sample_departure, precision=lax.Precision.HIGHEST
    )
    mode_coef = mode_coef.reshape(KV, KH, layer_tally, band_width, lat_rows)
    inc_part = (
        jnp.einsum(
            "al,bij,ablij->lij", vert_modes, horiz_modes, mode_coef, precision=lax.Precision.HIGHEST
        )
        * norm_scale
    )
    posterior_adjustment = lax.psum(inc_part, "mem")
    return (prognostic_vector, sample_centroid + posterior_adjustment)


def choose(*args):
    mem_dev, layers, width, lats = args[0].shape
    n_lon = lax.axis_size("lon")
    n_mem = lax.axis_size("mem")
    fits = (
        mem_dev == 8
        and layers == 4
        and n_mem == layers
        and n_lon == 8
        and width % 8 == 0
        and width > 16
        and lats == 256
        and args[5].shape[0] % (GROUPS * PIECE) == 0
    )
    return fast_device(*args) if fits else per_device(*args)


def solution(mesh):
    placed = (
        P("mem", None, "lon", None),
        P(None, "lon", None),
        P(None, "lon", None),
        P(),
        P(None, "lon", None),
        P("lon"),
        P("lon"),
        P("lon"),
        P("lon"),
    )
    return jax.shard_map(
        choose,
        mesh=mesh,
        in_specs=placed,
        out_specs=(P("mem", None, "lon", None), P(None, "lon", None)),
        check_vma=False,
    )
```
